32 devices in a mesh: group: 2 (over x), ingroup: 4 (over y, core), hid: 4 (over z).
Axes of the slice: x: 2, y: 2, z: 4, core: 2. Of those that a mesh axis runs over, the one named last changes fastest.
Arguments:
- tokens: bfloat16 [128, 2048], P(('group', 'hid')), may hold values from -6 to 6
- grad_mixed: bfloat16 [128, 2048], P(('group', 'hid')), may hold values from -6 to 6
- expert_ids: int32 [128, 6], P(('group', 'hid')), may hold values from 0 to 63, all different within a row; in each aligned block of 16 rows (0 to 15, 16 to 31, ...) at most 2 rows name the same one
- gate_weight: float32 [128, 6], P(('group', 'hid')), may hold values from 0.05 to 1
- w_gate: bfloat16 [64, 2048, 1408], P('hid', None, 'ingroup'), may hold values from -0.125 to 0.125
- w_up: bfloat16 [64, 2048, 1408], P('hid', None, 'ingroup'), may hold values from -0.125 to 0.125
- w_down: bfloat16 [64, 1408, 2048], P('hid', 'ingroup'), may hold values from -0.15625 to 0.15625
Outputs:
- mixed: bfloat16 [128, 2048], P(('group', 'hid'), 'ingroup')
- grad_tokens: bfloat16 [128, 2048], P(('group', 'hid'), 'ingroup')
- grad_gate: float32 [64, 2048, 1408], P('hid', 'group', 'ingroup')
- grad_up: float32 [64, 2048, 1408], P('hid', 'group', 'ingroup')
- grad_down: float32 [64, 1408, 2048], P('hid', 'ingroup', 'group')
The draws below stay inside these ranges and needn't reach their ends.
Inputs may be any that keep to these rules, and one draw needn't show every extreme that they name: `expert_ids`: each row names 6 different experts. Among the 16 tokens of one index of group and hid (aligned blocks of rows), no expert is named more than 2 times, and that bound is reached.
All inputs are finite; a program needn't handle non-finite values.
Results may differ from the reference program's by a relative error of at most 0.015.
Values may be sent and summed in bfloat16 or wider, within the bound.
No kernel may reach another device: no remote copies, remote signals or barrier semaphores. Data moves between devices by JAX's collectives and lax.ppermute only.
A program may use at most 256 MiB of HBM per device.

```python
import math
import jax
import jax.numpy as jnp
import numpy as np
from jax import lax

D = 2048
FF = 1408
EXPERTS = 64
TOP = 6
TOK_DEV = 16
CAP = 2
TOKENS = 128
N_GROUP = 2
N_INGROUP = 4
N_HID = 4


def levels(stream_key, extent, pieces, low, top_value):
    def one(position, shards_of):
        steps = jax.random.uniform(jax.random.fold_in(jax.random.fold_in(stream_key, 6), position), (shards_of,), jnp.float32, low / len(pieces), top_value / len(pieces))
        return jnp.repeat(jnp.exp(steps), extent[position] // shards_of).reshape((-1,) + (1,) * (len(extent) - position - 1))

    level = one(*pieces[0])
    for cut in pieces[1:]:
        level = level * one(*cut)
    return level


def deal_out(stream_key, own, number, rows, amount, top, bound, slope):
    sequence = jax.random.permutation(stream_key, amount)
    packed, ordinary = load_shares(amount, rows * top, bound, slope, True), load_shares(amount, rows * top, bound, slope, False)
    places = jnp.arange(amount)

    def named(lengths, rotation):
        used = int((lengths > 0).sum())
        fixed = max(1, used // 4)
        moved = fixed + (places - fixed + rotation * (used - fixed)) % max(1, amount - fixed)
        return jnp.zeros((amount,), jnp.int32).at[sequence[jnp.where(places < fixed, places, moved)]].set(jnp.asarray(lengths, jnp.int32))

    lengths = jnp.where(number % 4 == 0, named(packed, number // 4), named(ordinary, number - number // 4 - 1))
    mixed = jax.random.permutation(jax.random.fold_in(own, 3), amount)
    source_of, taker = mixed[0:amount // 2 * 2:2], mixed[1:amount // 2 * 2:2]
    slack = jnp.minimum(lengths[source_of] - 1, bound - lengths[taker]) // 2
    slack = jnp.where((source_of == sequence[0]) | (taker == sequence[0]) | (lengths[taker] == 0), 0, jnp.maximum(slack, 0))
    moved = jax.random.randint(jax.random.fold_in(own, 4), (amount // 2,), 0, 1 << 20) % (slack + 1)
    lengths = lengths.at[source_of].add(-moved).at[taker].add(moved)
    items = jnp.searchsorted(jnp.cumsum(lengths), jnp.arange(rows * top), side="right").astype(jnp.int32)
    table = items.reshape(top, rows).T
    table = table[jax.random.permutation(jax.random.fold_in(own, 1), rows)]
    rotation = jax.random.randint(jax.random.fold_in(own, 2), (rows, 1), 0, top)
    return jnp.take_along_axis(table, (jnp.arange(top)[None, :] + rotation) % top, axis=1)


def load_shares(amount, total, bound, lean, full):
    portions = [(1 << 20) // math.isqrt(grade ** lean) + 1 for grade in range(1, amount + 1)]
    largest = bound if full else min(bound, max(-(-total // amount), total * portions[0] // sum(portions)))
    least = 1 if total - largest >= amount - 1 else 0
    counts, surplus = [largest] + [least] * (amount - 1), total - largest - least * (amount - 1)
    while surplus > 0:
        candidates = [i for i in range(1, amount) if counts[i] < largest] or [i for i in range(1, amount) if counts[i] < bound]
        mass, remaining = sum([portions[i] for i in candidates]), surplus
        for i in candidates:
            addition = min(bound - counts[i], max(1, remaining * portions[i] // mass), surplus)
            counts[i] = counts[i] + addition
            surplus = surplus - addition
    return np.array(counts)


def gaussian(own_key, dims, deviation, most, pieces=(), held_as=jnp.bfloat16):
    array = jax.random.normal(own_key, dims, jnp.float32) * deviation
    if len(pieces) > 0:
        array = levels(own_key, dims, pieces, -0.22, 0.18) * array
    return jnp.clip(array, min=-most, max=most).astype(held_as)


def setup_inputs(seed: int = 0) -> dict:
    key_of = jax.random.split(jax.random.key(seed), 8)
    tokens = gaussian(key_of[0], (TOKENS, D), 1.0, 6.0, ((0, 8),))
    grad_mixed = gaussian(key_of[1], (TOKENS, D), 1.0, 6.0, ((0, 8),))
    expert_ids_keys = jax.random.split(jax.random.fold_in(key_of[2], 1), TOKENS // TOK_DEV)
    expert_ids_turns = jax.random.permutation(jax.random.fold_in(key_of[2], 3), TOKENS // TOK_DEV)
    expert_ids = jax.vmap(lambda own, number: deal_out(jax.random.fold_in(key_of[2], 2), own, number, TOK_DEV, EXPERTS, TOP, CAP, 2))(expert_ids_keys, expert_ids_turns).reshape((TOKENS, TOP))
    gate_weight = jnp.clip(jnp.exp(math.log(1.0) - 2.9957323 * jax.random.uniform(key_of[3], (TOKENS, TOP), jnp.float32) ** levels(key_of[3], (TOKENS, TOP), ((0, 8),), -0.2, 0.2)), 0.05, 1.0)
    w_gate = gaussian(key_of[4], (EXPERTS, D, FF), D ** -0.5, 0.125, ((0, 4), (2, 4)))
    w_up = gaussian(key_of[5], (EXPERTS, D, FF), D ** -0.5, 0.125, ((0, 4), (2, 4)))
    w_down = gaussian(key_of[6], (EXPERTS, FF, D), FF ** -0.5, 0.15625, ((0, 4), (1, 4)))
    return {"tokens": tokens, "grad_mixed": grad_mixed, "expert_ids": expert_ids, "gate_weight": gate_weight, "w_gate": w_gate, "w_up": w_up, "w_down": w_down}


def slot_tables(expert_ids, gate_weight):
    blocks = expert_ids.shape[0] // TOK_DEV
    per_block = TOK_DEV * TOP
    flat = expert_ids.reshape(blocks, per_block)
    onehot = (flat[:, :, None] == jnp.arange(EXPERTS, dtype=jnp.int32)[None, None, :]).astype(jnp.int32)
    rank = jnp.sum((jnp.cumsum(onehot, axis=1) - onehot) * onehot, axis=2).astype(jnp.int32)
    block_ids = jnp.arange(blocks, dtype=jnp.int32)[:, None]
    group_of = jnp.broadcast_to(block_ids // N_HID, flat.shape).astype(jnp.int32)
    row_index = ((block_ids % N_HID) * CAP + rank).astype(jnp.int32)
    token_index = (jnp.arange(blocks * per_block, dtype=jnp.int32) // TOP).reshape(blocks, per_block)
    rows_group = N_HID * CAP
    token_of = jnp.zeros((EXPERTS, N_GROUP, rows_group), jnp.int32).at[flat, group_of, row_index].set(token_index)
    live_of = jnp.zeros((EXPERTS, N_GROUP, rows_group), jnp.float32).at[flat, group_of, row_index].set(1.0)
    gate_of = jnp.zeros((EXPERTS, N_GROUP, rows_group), jnp.float32).at[flat, group_of, row_index].set(
        gate_weight.reshape(blocks, per_block))
    return flat, group_of, row_index, token_of, live_of, gate_of


def group_terms(left, right):
    partial_value = jnp.einsum("gmp,gmq->gpq",
                         left.reshape(N_GROUP, -1, left.shape[1]).astype(jnp.float32),
                         right.reshape(N_GROUP, -1, right.shape[1]).astype(jnp.float32))
    partial_value = lax.optimization_barrier(partial_value.astype(jnp.bfloat16))
    return jnp.sum(partial_value.astype(jnp.float32), axis=0)


def reference(tokens, grad_mixed, expert_ids, gate_weight, w_gate, w_up, w_down):
    flat, group_of, row_index, token_of, live_of, gate_of = slot_tables(expert_ids, gate_weight)
    slice_width = FF // N_INGROUP
    width = tokens.shape[1]
    rows_all = N_GROUP * N_HID * CAP

    def expert(inputs):
        token_idx, live, gates, wgate, wup, wdown = inputs
        token_flat = token_idx.reshape(rows_all)
        live_flat = live.reshape(rows_all)
        gate_flat = gates.reshape(rows_all)
        x_rows = jnp.where(live_flat[:, None] > 0.5, tokens[token_flat], jnp.zeros((), jnp.bfloat16))
        gated = (gate_flat[:, None] * grad_mixed[token_flat].astype(jnp.float32)).astype(jnp.bfloat16)
        gate_pre = jnp.dot(x_rows, wgate, preferred_element_type=jnp.float32)
        up_pre = jnp.dot(x_rows, wup, preferred_element_type=jnp.float32)
        sigmoid_gate = jax.nn.sigmoid(gate_pre)
        silu = gate_pre * sigmoid_gate
        hidden = (silu * up_pre).astype(jnp.bfloat16)
        parts = jnp.einsum("mjh,jhd->jmd", hidden.reshape(rows_all, N_INGROUP, slice_width).astype(jnp.float32),
                           wdown.reshape(N_INGROUP, slice_width, width).astype(jnp.float32))
        parts = lax.optimization_barrier(parts.astype(jnp.bfloat16))
        out_rows = jnp.sum(parts.astype(jnp.float32), axis=0).astype(jnp.bfloat16)
        d_hidden = jnp.dot(gated, wdown.T, preferred_element_type=jnp.float32)
        d_up = (d_hidden * silu).astype(jnp.bfloat16)
        d_gate = (d_hidden * up_pre * sigmoid_gate * (1.0 + gate_pre * (1.0 - sigmoid_gate))).astype(jnp.bfloat16)
        g_down = group_terms(hidden, gated)
        g_gate = group_terms(x_rows, d_gate)
        g_up = group_terms(x_rows, d_up)
        back = jnp.einsum("mjh,djh->jmd", d_gate.reshape(rows_all, N_INGROUP, slice_width).astype(jnp.float32),
                          wgate.reshape(width, N_INGROUP, slice_width).astype(jnp.float32))
        back = back + jnp.einsum("mjh,djh->jmd", d_up.reshape(rows_all, N_INGROUP, slice_width).astype(jnp.float32),
                                 wup.reshape(width, N_INGROUP, slice_width).astype(jnp.float32))
        back = lax.optimization_barrier(back.astype(jnp.bfloat16))
        in_rows = jnp.sum(back.astype(jnp.float32), axis=0).astype(jnp.bfloat16)
        return out_rows, in_rows, g_gate, g_up, g_down

    out_rows, in_rows, grad_gate, grad_up, grad_down = lax.map(
        expert, (token_of, live_of, gate_of, w_gate, w_up, w_down))
    out_rows = out_rows.reshape(EXPERTS, N_GROUP, N_HID * CAP, width)
    in_rows = in_rows.reshape(EXPERTS, N_GROUP, N_HID * CAP, width)
    picked_out = out_rows[flat, group_of, row_index].reshape(tokens.shape[0], TOP, width)
    picked_in = in_rows[flat, group_of, row_index].reshape(tokens.shape[0], TOP, width)
    mixed = jnp.sum(gate_weight[:, :, None] * picked_out.astype(jnp.float32), axis=1).astype(jnp.bfloat16)
    grad_tokens = jnp.sum(picked_in.astype(jnp.float32), axis=1).astype(jnp.bfloat16)
    return mixed, grad_tokens, grad_gate, grad_up, grad_down
```

```python
import functools

import jax
import jax.numpy as jnp
from jax import lax
from jax.experimental import pallas as pl
from jax.experimental.pallas import tpu as pltpu
from jax.sharding import PartitionSpec as P

TOP = 6


def plain(tokens, grad_mixed, expert_ids, gate_weight, w_gate, w_up, w_down):
    tok_count = tokens.shape[0]
    width = tokens.shape[1]
    n_hid = lax.axis_size("hid")
    exp_dev = w_gate.shape[0]
    experts_all = exp_dev * n_hid
    capacity = tok_count // 8
    slots_total = experts_all * capacity
    flat = expert_ids.reshape(tok_count * TOP)
    onehot = (flat[:, None] == jnp.arange(experts_all, dtype=jnp.int32)[None, :]).astype(jnp.int32)
    rank = jnp.sum((jnp.cumsum(onehot, axis=0) - onehot) * onehot, axis=1)
    owner_idx = flat // exp_dev
    local_idx = flat % exp_dev
    slot = (local_idx * n_hid + owner_idx) * capacity + rank
    token_index = jnp.arange(tok_count * TOP, dtype=jnp.int32) // TOP
    token_of = jnp.zeros((slots_total,), jnp.int32).at[slot].set(token_index)
    live_of = jnp.zeros((slots_total,), jnp.bool_).at[slot].set(True)
    gate_of = (
        jnp.zeros((slots_total,), jnp.float32).at[slot].set(gate_weight.reshape(tok_count * TOP))
    )
    send_x = jnp.where(live_of[:, None], tokens[token_of], jnp.zeros((), jnp.bfloat16))
    send_g = (gate_of[:, None] * grad_mixed[token_of].astype(jnp.float32)).astype(jnp.bfloat16)
    shape_whole = (exp_dev, n_hid, capacity, width)
    recv_x, recv_g = (
        lax.all_to_all(send_x.reshape(shape_whole), "hid", split_axis=1, concat_axis=1, tiled=True),
        lax.all_to_all(send_g.reshape(shape_whole), "hid", split_axis=1, concat_axis=1, tiled=True),
    )
    rows = n_hid * capacity
    x_rows = recv_x.reshape(exp_dev, rows, width)
    gated = recv_g.reshape(exp_dev, rows, width)
    gate_pre = jnp.einsum("emd,edh->emh", x_rows, w_gate, preferred_element_type=jnp.float32)
    up_pre = jnp.einsum("emd,edh->emh", x_rows, w_up, preferred_element_type=jnp.float32)
    sigmoid_gate = jax.nn.sigmoid(gate_pre)
    silu = gate_pre * sigmoid_gate
    hidden = (silu * up_pre).astype(jnp.bfloat16)
    out_part = jnp.einsum("emh,ehd->emd", hidden, w_down, preferred_element_type=jnp.float32)
    d_hidden = jnp.einsum("emd,ehd->emh", gated, w_down, preferred_element_type=jnp.float32)
    d_up = (d_hidden * silu).astype(jnp.bfloat16)
    d_gate = (d_hidden * up_pre * sigmoid_gate * (1.0 + gate_pre * (1.0 - sigmoid_gate))).astype(
        jnp.bfloat16
    )
    term_down = jnp.einsum("emh,emd->ehd", hidden, gated, preferred_element_type=jnp.float32)
    term_gate = jnp.einsum("emd,emh->edh", x_rows, d_gate, preferred_element_type=jnp.float32)
    term_up = jnp.einsum("emd,emh->edh", x_rows, d_up, preferred_element_type=jnp.float32)
    in_part = jnp.einsum("emh,edh->emd", d_gate, w_gate, preferred_element_type=jnp.float32)
    in_part = in_part + jnp.einsum("emh,edh->emd", d_up, w_up, preferred_element_type=jnp.float32)
    grad_gate, grad_up, grad_down = (
        lax.psum_scatter(
            term_gate.astype(jnp.bfloat16), "group", scatter_dimension=1, tiled=True
        ).astype(jnp.float32),
        lax.psum_scatter(
            term_up.astype(jnp.bfloat16), "group", scatter_dimension=1, tiled=True
        ).astype(jnp.float32),
        lax.psum_scatter(
            term_down.astype(jnp.bfloat16), "group", scatter_dimension=2, tiled=True
        ).astype(jnp.float32),
    )
    out_share, in_share = (
        lax.psum_scatter(
            out_part.astype(jnp.bfloat16), "ingroup", scatter_dimension=2, tiled=True
        ).astype(jnp.float32),
        lax.psum_scatter(
            in_part.astype(jnp.bfloat16), "ingroup", scatter_dimension=2, tiled=True
        ).astype(jnp.float32),
    )
    narrow = out_share.shape[2]
    out_share = out_share.astype(jnp.bfloat16)
    in_share = in_share.astype(jnp.bfloat16)
    back_shape = (exp_dev, n_hid, capacity, narrow)
    home_out, home_in = (
        lax.all_to_all(
            out_share.reshape(back_shape), "hid", split_axis=1, concat_axis=1, tiled=True
        ),
        lax.all_to_all(
            in_share.reshape(back_shape), "hid", split_axis=1, concat_axis=1, tiled=True
        ),
    )
    picked_out = home_out.reshape(slots_total, narrow)[slot].reshape(tok_count, TOP, narrow)
    picked_in = home_in.reshape(slots_total, narrow)[slot].reshape(tok_count, TOP, narrow)
    mixed = jnp.sum(gate_weight[:, :, None] * picked_out.astype(jnp.float32), axis=1).astype(
        jnp.bfloat16
    )
    grad_tokens = jnp.sum(picked_in.astype(jnp.float32), axis=1).astype(jnp.bfloat16)
    return (mixed, grad_tokens, grad_gate, grad_up, grad_down)


def middle_kernel(sizes, scal, u_ref, v_ref, wg_ref, wu_ref, wd_ref,
                  part_ref, act_ref, xs_ref, gs_ref,
                  x_scr, g_scr, c_scr, ct_scr, wbuf, acc_o, acc_i, act_scr, sem):
    n_group, n_ingroup, n_hid, tok, experts, half, cap = sizes
    ff, width = wbuf.shape[2], wbuf.shape[3]
    exp_own = wbuf.shape[1]
    rows = n_group * n_hid * tok
    wide = width // 2
    g, i, h = scal[0], scal[1], scal[2]
    core = lax.rem(i, 2)
    base = g * exp_own

    def fetch(e, k, ref):
        return pltpu.make_async_copy(ref.at[base + e], wbuf.at[k, e], sem.at[k, e])

    for e in range(exp_own):
        for k, ref in enumerate((wg_ref, wu_ref, wd_ref)):
            fetch(e, k, ref).start()

    for ref, part in ((u_ref, core), (v_ref, 1 - core)):
        for s in range(n_group):
            for d in range(n_hid):
                block = lax.rem(g + s, n_group) * n_hid + lax.rem(h - d + n_hid, n_hid)
                at = pl.ds(pl.multiple_of(block * tok, tok), tok)
                msg = s * n_hid + d
                x_scr[part, at, :] = ref[msg, :, :wide]
                g_scr[part, at, :] = ref[msg, :, wide:2 * wide]
                c_scr[part, at, :] = ref[msg, :, 2 * wide:].astype(jnp.float32)

    lanes = c_scr.shape[2]
    first, second = c_scr[0], c_scr[1]
    weight = first + pltpu.roll(first, lanes - experts, 1) + second
    lane = lax.broadcasted_iota(jnp.int32, (rows, lanes), 1)
    weight = jnp.where(lane < experts, weight, 0.0)
    routed = (weight > 0).astype(jnp.bfloat16)
    row_a = lax.broadcasted_iota(jnp.int32, (rows, rows), 0)
    row_b = lax.broadcasted_iota(jnp.int32, (rows, rows), 1)
    before = ((row_a // tok == row_b // tok) & (row_b < row_a)).astype(jnp.bfloat16)
    rank = jnp.dot(before, routed, preferred_element_type=jnp.float32)
    block_of = (lax.broadcasted_iota(jnp.int32, (rows, lanes), 0) // tok).astype(jnp.float32)
    slot = jnp.where(weight > 0, rank + cap * block_of, -1.0)
    ct_scr[...] = weight.T
    slots = n_group * n_hid * cap
    spread_e = lax.broadcasted_iota(jnp.int32, (lanes, exp_own * slots), 0)
    spread_l = lax.broadcasted_iota(jnp.int32, (lanes, exp_own * slots), 1)
    lane_s = lax.broadcasted_iota(jnp.int32, (rows, exp_own * slots), 1)
    picks = []
    for which in range(n_group):
        owner = h * (exp_own * n_group) + lax.rem(g + which, n_group) * exp_own
        spread = (spread_e == owner + spread_l // slots).astype(jnp.bfloat16)
        slot_l = jnp.dot(slot.astype(jnp.bfloat16), spread, preferred_element_type=jnp.float32)
        pick = (slot_l == (lane_s % slots).astype(jnp.float32)).astype(jnp.float32)
        pick_t = pick.T.astype(jnp.bfloat16)
        picks.append(pick.astype(jnp.bfloat16))
        xs_ref[which] = jnp.dot(pick_t, x_scr[g], preferred_element_type=jnp.float32).astype(jnp.bfloat16)
        gs_ref[which] = jnp.dot(pick_t, g_scr[g], preferred_element_type=jnp.float32).astype(jnp.bfloat16)

    acc_o[...] = jnp.zeros_like(acc_o)
    acc_i[...] = jnp.zeros_like(acc_i)
    act_scr[...] = jnp.zeros_like(act_scr)
    pair = 2
    nt = (((1,), (1,)), ((), ()))
    tn = (((0,), (0,)), ((), ()))

    def both(k, e0, tok_scr):
        w = wbuf[k, pl.ds(e0, pair)].reshape(pair * ff, width)
        return (lax.dot_general(w[:, :wide], tok_scr[0], nt, preferred_element_type=jnp.float32)
                + lax.dot_general(w[:, wide:], tok_scr[1], nt, preferred_element_type=jnp.float32))

    def step(j, carry):
        e0 = j * pair
        for e in range(pair):
            for k, ref in enumerate((wg_ref, wu_ref, wd_ref)):
                fetch(e0 + e, k, ref).wait()
        gate = both(0, e0, x_scr).reshape(pair, ff, rows)
        up = both(1, e0, x_scr).reshape(pair, ff, rows)
        back = both(2, e0, g_scr).reshape(pair, ff, rows)
        ct = ct_scr[pl.ds(h * (exp_own * n_group) + base + e0, pair), :].reshape(pair, 1, rows)
        sig = jax.nn.sigmoid(gate)
        silu = gate * sig
        d_hid = back * ct
        hid = (silu * up * ct).astype(jnp.bfloat16)
        d_up = (d_hid * silu).astype(jnp.bfloat16)
        d_gate = (d_hid * up * sig * (1.0 + gate * (1.0 - sig))).astype(jnp.bfloat16)
        where_l = lax.broadcasted_iota(jnp.int32, (ff, exp_own * slots), 1) // slots
        for k, val in enumerate((d_gate, d_up, hid)):
            for e in range(pair):
                packed = jnp.dot(val[e], picks[0], preferred_element_type=jnp.float32)
                act_scr[k] = jnp.where(where_l == e0 + e, packed, act_scr[k])
        w = [wbuf[k, pl.ds(e0, pair)].reshape(pair * ff, width) for k in range(3)]
        flat = [val.reshape(pair * ff, rows) for val in (d_gate, d_up, hid)]
        acc_o[...] += lax.dot_general(flat[2], w[2], tn, preferred_element_type=jnp.float32)
        acc_i[...] += (lax.dot_general(flat[0], w[0], tn, preferred_element_type=jnp.float32)
                       + lax.dot_general(flat[1], w[1], tn, preferred_element_type=jnp.float32))
        return carry

    lax.fori_loop(0, exp_own // pair, step, 0)
    act_ref[...] = act_scr[...].astype(jnp.bfloat16)
    narrow = width // n_ingroup
    for q in range(n_ingroup):
        for b in range(n_group * n_hid):
            rel_i = q ^ i
            rel_b = b ^ (g * n_hid + h)
            cols = slice(q * narrow, (q + 1) * narrow)
            at = slice(b * tok, (b + 1) * tok)
            part_ref[lax.rem(rel_i, 2), rel_i // 2, rel_b, 0] = acc_o[at, cols].astype(jnp.bfloat16)
            part_ref[lax.rem(rel_i, 2), rel_i // 2, rel_b, 1] = acc_i[at, cols].astype(jnp.bfloat16)


def grad_kernel(slots, first, scal, act_ref, xs_ref, gs_ref, *refs):
    gate_ref, up_ref, down_ref = refs[-3:]
    j = pl.program_id(0) + first
    where_l = lax.broadcasted_iota(jnp.int32, act_ref.shape[1:], 1) // slots
    for k, (out, right) in enumerate(((gate_ref, xs_ref), (up_ref, xs_ref), (down_ref, gs_ref))):
        left = jnp.where(where_l == j, act_ref[k], jnp.zeros((), jnp.bfloat16))
        out[0] = jnp.dot(left, right[...], preferred_element_type=jnp.float32)


def grads(scal, act, xs, gs, which, first, count, before, experts, n_group, slots):
    ff = act.shape[1]
    wide = xs.shape[2]
    own = experts // n_group

    def out_map(j, scal):
        return (lax.rem(scal[0] + which, n_group) * own + first + j, 0, 0)

    full = jax.ShapeDtypeStruct((experts, ff, wide), jnp.float32)
    n_before = 3 if before is not None else 0
    return pl.pallas_call(
        functools.partial(grad_kernel, slots, first),
        out_shape=[full] * 3,
        grid_spec=pltpu.PrefetchScalarGridSpec(
            num_scalar_prefetch=1,
            grid=(count,),
            in_specs=[
                pl.BlockSpec(act.shape, lambda j, scal: (0, 0, 0)),
                pl.BlockSpec((None,) + xs.shape[1:], lambda j, scal: (which, 0, 0)),
                pl.BlockSpec((None,) + gs.shape[1:], lambda j, scal: (which, 0, 0)),
            ] + [pl.BlockSpec(memory_space=pl.ANY)] * n_before,
            out_specs=[pl.BlockSpec((1, ff, wide), out_map)] * 3,
        ),
        input_output_aliases={4 + k: k for k in range(n_before)},
        compiler_params=pltpu.CompilerParams(vmem_limit_bytes=40 << 20),
        cost_estimate=pl.CostEstimate(
            flops=count * 3 * 2 * ff * act.shape[2] * wide,
            bytes_accessed=count * 3 * ff * wide * 4, transcendentals=0),
        name="weight_grads",
    )(scal, act, xs, gs, *(before or ()))


def swap(x, axis, bit):
    n = lax.axis_size(axis)
    return lax.ppermute(x, axis, [(k, k ^ bit) for k in range(n)])


def shards(tokens, grad_mixed, expert_ids, gate_weight, w_gate, w_up, w_down):
    tok, width = tokens.shape
    n_group, n_ingroup, n_hid = (lax.axis_size(a) for a in ("group", "ingroup", "hid"))
    exp_dev, ff = w_down.shape[0], w_down.shape[1]
    experts = exp_dev * n_hid
    cap = tok // 8
    own = exp_dev // n_group
    rows = n_group * n_hid * tok
    slots = n_group * n_hid * cap
    if not (n_group == 2 and n_ingroup == 4 and exp_dev % (2 * n_group) == 0 and n_hid & (n_hid - 1) == 0
            and rows == 128 and own * slots == 128 and 2 * experts <= 128):
        return plain(tokens, grad_mixed, expert_ids, gate_weight, w_gate, w_up, w_down)
    g, i, h = (lax.axis_index(a) for a in ("group", "ingroup", "hid"))
    scal = jnp.stack([g, i, h]).astype(jnp.int32)
    core = lax.rem(i, 2)
    half = width // 2
    table = jnp.sum(jnp.where(expert_ids[:, :, None] == jnp.arange(experts, dtype=jnp.int32)[None, None, :],
                              gate_weight[:, :, None], 0.0), axis=1)
    hi = lax.reduce_precision(table, 8, 7)
    mid = lax.reduce_precision(table - hi, 8, 7)
    low = lax.reduce_precision(table - hi - mid, 8, 7)
    zero = jnp.zeros_like(hi)
    terms = jnp.where(core == 0, jnp.concatenate([hi, mid], 1), jnp.concatenate([low, zero], 1))
    message = jnp.concatenate([
        lax.dynamic_slice_in_dim(tokens, core * half, half, 1),
        lax.dynamic_slice_in_dim(grad_mixed, core * half, half, 1),
        terms.astype(jnp.bfloat16)], axis=1)
    line = [message] + [lax.ppermute(message, "hid", [(k, (k + d) % n_hid) for k in range(n_hid)])
                        for d in range(1, n_hid)]
    line = jnp.stack(line)
    mine = jnp.concatenate([line, swap(line, "group", 1)])
    theirs = swap(mine, "ingroup", 1)
    wg, wu = jnp.swapaxes(w_gate, 1, 2), jnp.swapaxes(w_up, 1, 2)
    narrow = width // n_ingroup
    any_space = pl.BlockSpec(memory_space=pl.ANY)
    vmem = pl.BlockSpec(memory_space=pltpu.VMEM)
    lanes = message.shape[1] - 2 * half
    part, act, xs, gs = pl.pallas_call(
        functools.partial(middle_kernel, (n_group, n_ingroup, n_hid, tok, experts, half, cap)),
        out_shape=[
            jax.ShapeDtypeStruct((2, n_ingroup // 2, n_group * n_hid, 2, tok, narrow), jnp.bfloat16),
            jax.ShapeDtypeStruct((3, ff, own * slots), jnp.bfloat16),
            jax.ShapeDtypeStruct((n_group, own * slots, half), jnp.bfloat16),
            jax.ShapeDtypeStruct((n_group, own * slots, half), jnp.bfloat16),
        ],
        in_specs=[pl.BlockSpec(memory_space=pltpu.SMEM), vmem, vmem, any_space, any_space, any_space],
        out_specs=[vmem] * 4,
        scratch_shapes=[
            pltpu.VMEM((2, rows, half), jnp.bfloat16),
            pltpu.VMEM((2, rows, half), jnp.bfloat16),
            pltpu.VMEM((2, rows, lanes), jnp.float32),
            pltpu.VMEM((lanes, rows), jnp.float32),
            pltpu.VMEM((3, own, ff, width), jnp.bfloat16),
            pltpu.VMEM((rows, width), jnp.float32),
            pltpu.VMEM((rows, width), jnp.float32),
            pltpu.VMEM((3, ff, own * slots), jnp.float32),
            pltpu.SemaphoreType.DMA((3, own)),
        ],
        compiler_params=pltpu.CompilerParams(vmem_limit_bytes=62 << 20),
        cost_estimate=pl.CostEstimate(flops=6 * 2 * own * ff * width * rows,
                                      bytes_accessed=3 * own * ff * width * 2, transcendentals=own * ff * rows),
        name="experts",
    )(scal, mine, theirs, wg, wu, w_down)
    act_other = swap(act, "group", 1)
    args = (exp_dev, n_group, slots)
    now = part[0] + swap(part[1], "ingroup", 1)
    now = now[0] + swap(now[1], "ingroup", 2)
    span = n_group * n_hid // 2
    now = now[:span] + swap(now[span:], "group", 1)
    bit = n_hid // 2
    while bit:
        now = now[:bit] + swap(now[bit:], "hid", bit)
        bit //= 2
    out = grads(scal, act, xs, gs, 0, 0, own, None, *args)
    out = grads(scal, act_other, xs, gs, 1, 0, own, out, *args)
    return (now[0, 0], now[0, 1], jnp.swapaxes(out[0], 1, 2), jnp.swapaxes(out[1], 1, 2), out[2])


def solution(mesh):
    placed = (
        P(("group", "hid"), None),
        P(("group", "hid"), None),
        P(("group", "hid"), None),
        P(("group", "hid"), None),
        P("hid", None, "ingroup"),
        P("hid", None, "ingroup"),
        P("hid", "ingroup", None),
    )
    return jax.shard_map(
        shards,
        mesh=mesh,
        in_specs=placed,
        out_specs=(
            P(("group", "hid"), "ingroup"),
            P(("group", "hid"), "ingroup"),
            P("hid", "group", "ingroup"),
            P("hid", "group", "ingroup"),
            P("hid", "ingroup", "group"),
        ),
        check_vma=False,
    )
```

```python
import functools

import jax
import jax.numpy as jnp
from jax import lax
from jax.experimental import pallas as pl
from jax.experimental.pallas import tpu as pltpu
from jax.sharding import PartitionSpec as P

TOP = 6


def plain(tokens, grad_mixed, expert_ids, gate_weight, w_gate, w_up, w_down):
    tok_count = tokens.shape[0]
    width = tokens.shape[1]
    n_hid = lax.axis_size("hid")
    exp_dev = w_gate.shape[0]
    experts_all = exp_dev * n_hid
    capacity = tok_count // 8
    slots_total = experts_all * capacity
    flat = expert_ids.reshape(tok_count * TOP)
    onehot = (flat[:, None] == jnp.arange(experts_all, dtype=jnp.int32)[None, :]).astype(jnp.int32)
    rank = jnp.sum((jnp.cumsum(onehot, axis=0) - onehot) * onehot, axis=1)
    owner_idx = flat // exp_dev
    local_idx = flat % exp_dev
    slot = (local_idx * n_hid + owner_idx) * capacity + rank
    token_index = jnp.arange(tok_count * TOP, dtype=jnp.int32) // TOP
    token_of = jnp.zeros((slots_total,), jnp.int32).at[slot].set(token_index)
    live_of = jnp.zeros((slots_total,), jnp.bool_).at[slot].set(True)
    gate_of = (
        jnp.zeros((slots_total,), jnp.float32).at[slot].set(gate_weight.reshape(tok_count * TOP))
    )
    send_x = jnp.where(live_of[:, None], tokens[token_of], jnp.zeros((), jnp.bfloat16))
    send_g = (gate_of[:, None] * grad_mixed[token_of].astype(jnp.float32)).astype(jnp.bfloat16)
    shape_whole = (exp_dev, n_hid, capacity, width)
    recv_x, recv_g = (
        lax.all_to_all(send_x.reshape(shape_whole), "hid", split_axis=1, concat_axis=1, tiled=True),
        lax.all_to_all(send_g.reshape(shape_whole), "hid", split_axis=1, concat_axis=1, tiled=True),
    )
    rows = n_hid * capacity
    x_rows = recv_x.reshape(exp_dev, rows, width)
    gated = recv_g.reshape(exp_dev, rows, width)
    gate_pre = jnp.einsum("emd,edh->emh", x_rows, w_gate, preferred_element_type=jnp.float32)
    up_pre = jnp.einsum("emd,edh->emh", x_rows, w_up, preferred_element_type=jnp.float32)
    sigmoid_gate = jax.nn.sigmoid(gate_pre)
    silu = gate_pre * sigmoid_gate
    hidden = (silu * up_pre).astype(jnp.bfloat16)
    out_part = jnp.einsum("emh,ehd->emd", hidden, w_down, preferred_element_type=jnp.float32)
    d_hidden = jnp.einsum("emd,ehd->emh", gated, w_down, preferred_element_type=jnp.float32)
    d_up = (d_hidden * silu).astype(jnp.bfloat16)
    d_gate = (d_hidden * up_pre * sigmoid_gate * (1.0 + gate_pre * (1.0 - sigmoid_gate))).astype(
        jnp.bfloat16
    )
    term_down = jnp.einsum("emh,emd->ehd", hidden, gated, preferred_element_type=jnp.float32)
    term_gate = jnp.einsum("emd,emh->edh", x_rows, d_gate, preferred_element_type=jnp.float32)
    term_up = jnp.einsum("emd,emh->edh", x_rows, d_up, preferred_element_type=jnp.float32)
    in_part = jnp.einsum("emh,edh->emd", d_gate, w_gate, preferred_element_type=jnp.float32)
    in_part = in_part + jnp.einsum("emh,edh->emd", d_up, w_up, preferred_element_type=jnp.float32)
    grad_gate, grad_up, grad_down = (
        lax.psum_scatter(
            term_gate.astype(jnp.bfloat16), "group", scatter_dimension=1, tiled=True
        ).astype(jnp.float32),
        lax.psum_scatter(
            term_up.astype(jnp.bfloat16), "group", scatter_dimension=1, tiled=True
        ).astype(jnp.float32),
        lax.psum_scatter(
            term_down.astype(jnp.bfloat16), "group", scatter_dimension=2, tiled=True
        ).astype(jnp.float32),
    )
    out_share, in_share = (
        lax.psum_scatter(
            out_part.astype(jnp.bfloat16), "ingroup", scatter_dimension=2, tiled=True
        ).astype(jnp.float32),
        lax.psum_scatter(
            in_part.astype(jnp.bfloat16), "ingroup", scatter_dimension=2, tiled=True
        ).astype(jnp.float32),
    )
    narrow = out_share.shape[2]
    out_share = out_share.astype(jnp.bfloat16)
    in_share = in_share.astype(jnp.bfloat16)
    back_shape = (exp_dev, n_hid, capacity, narrow)
    home_out, home_in = (
        lax.all_to_all(
            out_share.reshape(back_shape), "hid", split_axis=1, concat_axis=1, tiled=True
        ),
        lax.all_to_all(
            in_share.reshape(back_shape), "hid", split_axis=1, concat_axis=1, tiled=True
        ),
    )
    picked_out = home_out.reshape(slots_total, narrow)[slot].reshape(tok_count, TOP, narrow)
    picked_in = home_in.reshape(slots_total, narrow)[slot].reshape(tok_count, TOP, narrow)
    mixed = jnp.sum(gate_weight[:, :, None] * picked_out.astype(jnp.float32), axis=1).astype(
        jnp.bfloat16
    )
    grad_tokens = jnp.sum(picked_in.astype(jnp.float32), axis=1).astype(jnp.bfloat16)
    return (mixed, grad_tokens, grad_gate, grad_up, grad_down)


def middle_kernel(sizes, places, scal, wg_ref, wu_ref, wd_ref, *refs):
    n_group, n_ingroup, n_hid, tok, experts, half, cap = sizes
    message_refs, refs = refs[:2 * len(places)], refs[2 * len(places):]
    keep_ref, send_ref, act_ref, xs_ref, gs_ref = refs[:5]
    x_scr, g_scr, c_scr, w_scr, pick_scr, wbuf, acc_o, acc_i, sem = refs[5:]
    ff, width = wbuf.shape[2], wbuf.shape[3]
    exp_own = wbuf.shape[1]
    rows = n_group * n_hid * tok
    wide = width // 2
    g, i, h = scal[0], scal[1], scal[2]
    core = lax.rem(i, 2)
    base = g * exp_own
    pair = 2

    def fetch(e, k, ref):
        return pltpu.make_async_copy(ref.at[base + e], wbuf.at[k, e], sem.at[k, e])

    for e0 in range(0, exp_own, pair):
        for k, ref in enumerate((wg_ref, wu_ref, wd_ref)):
            for e in range(pair):
                fetch(e0 + e, k, ref).start()

    for m, place in enumerate(places):
        for ref, part in ((message_refs[2 * m], core), (message_refs[2 * m + 1], 1 - core)):
            for at_msg, (s, d) in enumerate(place):
                block = lax.rem(g + s, n_group) * n_hid + lax.rem(h - d + n_hid, n_hid)
                at = pl.ds(pl.multiple_of(block * tok, tok), tok)
                cols = pl.ds(pl.multiple_of(part * wide, wide), wide)
                x_scr[at, cols] = ref[at_msg, :, :wide]
                g_scr[at, cols] = ref[at_msg, :, wide:2 * wide]
                c_scr[part, at, :] = ref[at_msg, :, 2 * wide:].astype(jnp.float32)

    lanes = c_scr.shape[2]
    first, second = c_scr[0], c_scr[1]
    weight = first + pltpu.roll(first, lanes - experts, 1) + second
    lane = lax.broadcasted_iota(jnp.int32, (rows, lanes), 1)
    weight = jnp.where(lane < experts, weight, 0.0)
    w_scr[...] = weight
    routed = (weight > 0).astype(jnp.bfloat16)
    row_a = lax.broadcasted_iota(jnp.int32, (rows, rows), 0)
    row_b = lax.broadcasted_iota(jnp.int32, (rows, rows), 1)
    before = ((row_a // tok == row_b // tok) & (row_b < row_a)).astype(jnp.bfloat16)
    rank = jnp.dot(before, routed, preferred_element_type=jnp.float32)
    block_of = (lax.broadcasted_iota(jnp.int32, (rows, lanes), 0) // tok).astype(jnp.float32)
    slot = jnp.where(weight > 0, rank + cap * block_of, -1.0)
    slots = n_group * n_hid * cap
    spread_e = lax.broadcasted_iota(jnp.int32, (lanes, exp_own * slots), 0)
    spread_l = lax.broadcasted_iota(jnp.int32, (lanes, exp_own * slots), 1)
    lane_s = lax.broadcasted_iota(jnp.int32, (rows, exp_own * slots), 1)
    for which in range(n_group):
        owner = h * (exp_own * n_group) + lax.rem(g + which, n_group) * exp_own
        spread = (spread_e == owner + spread_l // slots).astype(jnp.bfloat16)
        slot_l = jnp.dot(slot.astype(jnp.bfloat16), spread, preferred_element_type=jnp.float32)
        pick = (slot_l == (lane_s % slots).astype(jnp.float32)).astype(jnp.float32).T.astype(jnp.bfloat16)
        if which == 0:
            pick_scr[...] = pick
        xs_ref[which] = jnp.dot(pick, x_scr[:, pl.ds(pl.multiple_of(g * wide, wide), wide)],
                                preferred_element_type=jnp.float32).astype(jnp.bfloat16)
        gs_ref[which] = jnp.dot(pick, g_scr[:, pl.ds(pl.multiple_of(g * wide, wide), wide)],
                                preferred_element_type=jnp.float32).astype(jnp.bfloat16)

    acc_o[...] = jnp.zeros_like(acc_o)
    acc_i[...] = jnp.zeros_like(acc_i)
    nt = (((1,), (1,)), ((), ()))
    lane_f = lax.broadcasted_iota(jnp.int32, (rows, pair * ff), 1)

    def step(j, carry):
        e0 = j * pair
        w, pre = [], []
        for k, (ref, rows_of) in enumerate(((wg_ref, x_scr), (wu_ref, x_scr), (wd_ref, g_scr))):
            for e in range(pair):
                fetch(e0 + e, k, ref).wait()
            w.append(wbuf[k, pl.ds(e0, pair)].reshape(pair * ff, width))
            pre.append(lax.dot_general(rows_of[...], w[k], nt, preferred_element_type=jnp.float32))
        gate, up, back = pre
        at = h * (exp_own * n_group) + base + e0
        col = [jnp.sum(jnp.where(lane == at + e, w_scr[...], 0.0), axis=1, keepdims=True) for e in range(pair)]
        scale = jnp.where(lane_f < ff, col[0], col[1])
        sig = jax.nn.sigmoid(gate)
        silu = gate * sig
        d_hid = back * scale
        hid = (silu * up * scale).astype(jnp.bfloat16)
        d_up = (d_hid * silu).astype(jnp.bfloat16)
        d_gate = (d_hid * up * sig * (1.0 + gate * (1.0 - sig))).astype(jnp.bfloat16)
        pick = pick_scr[pl.ds(pl.multiple_of(e0 * slots, pair * slots), pair * slots), :]
        for k, val in enumerate((d_gate, d_up, hid)):
            packed = jnp.dot(pick, val, preferred_element_type=jnp.float32).astype(jnp.bfloat16)
            for e in range(pair):
                act_ref[k, pl.ds(pl.multiple_of((e0 + e) * slots, slots), slots), :] = packed[
                    e * slots:(e + 1) * slots, e * ff:(e + 1) * ff]
        acc_o[...] += jnp.dot(hid, w[2], preferred_element_type=jnp.float32)
        acc_i[...] += (jnp.dot(d_gate, w[0], preferred_element_type=jnp.float32)
                       + jnp.dot(d_up, w[1], preferred_element_type=jnp.float32))
        return carry

    lax.fori_loop(0, exp_own // pair, step, 0)
    narrow = width // n_ingroup
    for y in range(n_ingroup // 2):
        for b in range(n_group * n_hid):
            rel_y = y ^ (i // 2)
            rel_b = b ^ (g * n_hid + h)
            at = slice(b * tok, (b + 1) * tok)
            for k, acc in enumerate((acc_o, acc_i)):
                two = [acc[at, (2 * y + c) * narrow:(2 * y + c + 1) * narrow].astype(jnp.bfloat16) for c in range(2)]
                keep_ref[rel_y, rel_b, k] = jnp.where(core == 0, two[0], two[1])
                send_ref[rel_y, rel_b, k] = jnp.where(core == 0, two[1], two[0])


def add_kernel(keep_ref, got_ref, mark_ref, *out_refs):
    del mark_ref
    size = out_refs[0].shape[0]
    for k, out in enumerate(out_refs):
        at = slice(k * size, (k + 1) * size)
        out[...] = (keep_ref[at].astype(jnp.float32) + got_ref[at].astype(jnp.float32)).astype(out.dtype)


def add_halves(keep, got, mark):
    vmem = pl.BlockSpec(memory_space=pltpu.VMEM)
    n = 2 if keep.shape[0] > 1 else 1
    return pl.pallas_call(
        add_kernel,
        out_shape=[jax.ShapeDtypeStruct((keep.shape[0] // n,) + keep.shape[1:], keep.dtype)] * n,
        in_specs=[vmem, vmem, pl.BlockSpec(memory_space=pl.ANY)],
        out_specs=[vmem] * n,
        compiler_params=pltpu.CompilerParams(vmem_limit_bytes=4 << 20),
        cost_estimate=pl.CostEstimate(flops=keep.size, bytes_accessed=keep.size * 6, transcendentals=0),
        name="add_halves",
    )(keep, got, mark)


def grad_kernel(piece, slots, n_group, scal, act_ref, xs_ref, gs_ref, *refs):
    which, first, count = piece
    *outs, mark_ref, stage, sem = refs[-6:]
    mark_ref[...] = jnp.zeros_like(mark_ref)
    own = act_ref.shape[1] // slots
    base = lax.rem(scal[0] + which, n_group) * own + first
    tn = (((0,), (0,)), ((), ()))
    depth = stage.shape[0]

    def put(j, k):
        slot = lax.rem(j, depth)
        return pltpu.make_async_copy(stage.at[slot, k], outs[k].at[base + j], sem.at[slot, k])

    def step(j, carry):
        at = pl.ds(pl.multiple_of((first + j) * slots, slots), slots)
        for k, right in enumerate((xs_ref, xs_ref, gs_ref)):
            @pl.when(j >= depth)
            def _():
                put(j - depth, k).wait()
            stage[lax.rem(j, depth), k] = lax.dot_general(
                act_ref[k, at, :], right[which, at, :], tn, preferred_element_type=jnp.float32)
            put(j, k).start()
        return carry

    lax.fori_loop(0, count, step, 0)
    for j in range(max(0, count - depth), count):
        for k in range(3):
            put(j, k).wait()


def grads(scal, act, xs, gs, piece, out, after, shape, n_group, slots):
    ff, wide, count = act.shape[2], xs.shape[2], piece[2]
    depth = min(2, count)
    vmem, any_space = pl.BlockSpec(memory_space=pltpu.VMEM), pl.BlockSpec(memory_space=pl.ANY)
    return pl.pallas_call(
        functools.partial(grad_kernel, piece, slots, n_group),
        out_shape=[shape] * 3 + [jax.ShapeDtypeStruct((8, 128), jnp.float32)],
        in_specs=[pl.BlockSpec(memory_space=pltpu.SMEM)] + [vmem] * 3 + [any_space] * (4 if out else 1),
        out_specs=[any_space] * 3 + [vmem],
        scratch_shapes=[pltpu.VMEM((depth, 3, ff, wide), jnp.float32), pltpu.SemaphoreType.DMA((depth, 3))],
        input_output_aliases={5 + k: k for k in range(3)} if out else {},
        compiler_params=pltpu.CompilerParams(vmem_limit_bytes=12 << 20),
        cost_estimate=pl.CostEstimate(
            flops=count * 3 * 2 * ff * slots * wide,
            bytes_accessed=count * 3 * ff * wide * 4, transcendentals=0),
        name="weight_grads",
    )(scal, act, xs, gs, after, *(out or ()))


def swap(x, axis, bit):
    n = lax.axis_size(axis)
    return lax.ppermute(x, axis, [(k, k ^ bit) for k in range(n)])


def shards(tokens, grad_mixed, expert_ids, gate_weight, w_gate, w_up, w_down):
    tok, width = tokens.shape
    n_group, n_ingroup, n_hid = (lax.axis_size(a) for a in ("group", "ingroup", "hid"))
    exp_dev, ff = w_down.shape[0], w_down.shape[1]
    experts = exp_dev * n_hid
    cap = tok // 8
    own = exp_dev // n_group
    rows = n_group * n_hid * tok
    slots = n_group * n_hid * cap
    if not (n_group == 2 and n_ingroup == 4 and exp_dev % (2 * n_group) == 0 and n_hid & (n_hid - 1) == 0
            and rows == 128 and own * slots == 128 and 2 * experts <= 128):
        return plain(tokens, grad_mixed, expert_ids, gate_weight, w_gate, w_up, w_down)
    g, i, h = (lax.axis_index(a) for a in ("group", "ingroup", "hid"))
    scal = jnp.stack([g, i, h]).astype(jnp.int32)
    core = lax.rem(i, 2)
    half = width // 2
    table = jnp.sum(jnp.where(expert_ids[:, :, None] == jnp.arange(experts, dtype=jnp.int32)[None, None, :],
                              gate_weight[:, :, None], 0.0), axis=1)
    hi = lax.reduce_precision(table, 8, 7)
    mid = lax.reduce_precision(table - hi, 8, 7)
    low = lax.reduce_precision(table - hi - mid, 8, 7)
    zero = jnp.zeros_like(hi)
    terms = jnp.where(core == 0, jnp.concatenate([hi, mid], 1), jnp.concatenate([low, zero], 1))
    message = jnp.concatenate([
        lax.dynamic_slice_in_dim(tokens, core * half, half, 1),
        lax.dynamic_slice_in_dim(grad_mixed, core * half, half, 1),
        terms.astype(jnp.bfloat16)], axis=1)
    line = [message] + [lax.ppermute(message, "hid", [(k, (k + d) % n_hid) for k in range(n_hid)])
                        for d in range(1, n_hid)]
    messages, places = [], []
    for low in range(0, n_hid, n_hid // 2):
        group_of = range(low, low + n_hid // 2)
        mine = jnp.stack([line[d] for d in group_of])
        for s, block in enumerate((mine, swap(mine, "group", 1))):
            messages += [block, swap(block, "ingroup", 1)]
            places.append(tuple((s, d) for d in group_of))
    wg, wu = jnp.swapaxes(w_gate, 1, 2), jnp.swapaxes(w_up, 1, 2)
    narrow = width // n_ingroup
    any_space = pl.BlockSpec(memory_space=pl.ANY)
    vmem = pl.BlockSpec(memory_space=pltpu.VMEM)
    lanes = message.shape[1] - 2 * half
    keep, send, act, xs, gs = pl.pallas_call(
        functools.partial(middle_kernel, (n_group, n_ingroup, n_hid, tok, experts, half, cap), tuple(places)),
        out_shape=[
            jax.ShapeDtypeStruct((n_ingroup // 2, n_group * n_hid, 2, tok, narrow), jnp.bfloat16),
            jax.ShapeDtypeStruct((n_ingroup // 2, n_group * n_hid, 2, tok, narrow), jnp.bfloat16),
            jax.ShapeDtypeStruct((3, own * slots, ff), jnp.bfloat16),
            jax.ShapeDtypeStruct((n_group, own * slots, half), jnp.bfloat16),
            jax.ShapeDtypeStruct((n_group, own * slots, half), jnp.bfloat16),
        ],
        in_specs=[pl.BlockSpec(memory_space=pltpu.SMEM)] + [any_space] * 3 + [vmem] * len(messages),
        out_specs=[vmem] * 5,
        scratch_shapes=[
            pltpu.VMEM((rows, width), jnp.bfloat16),
            pltpu.VMEM((rows, width), jnp.bfloat16),
            pltpu.VMEM((2, rows, lanes), jnp.float32),
            pltpu.VMEM((rows, lanes), jnp.float32),
            pltpu.VMEM((own * slots, rows), jnp.bfloat16),
            pltpu.VMEM((3, own, ff, width), jnp.bfloat16),
            pltpu.VMEM((rows, width), jnp.float32),
            pltpu.VMEM((rows, width), jnp.float32),
            pltpu.SemaphoreType.DMA((3, own)),
        ],
        compiler_params=pltpu.CompilerParams(vmem_limit_bytes=46 << 20),
        cost_estimate=pl.CostEstimate(flops=6 * 2 * own * ff * width * rows,
                                      bytes_accessed=3 * own * ff * width * 2, transcendentals=own * ff * rows),
        name="experts",
    )(scal, wg, wu, w_down, *messages)
    grad_shape = jax.ShapeDtypeStruct((exp_dev, ff, width // n_group), jnp.float32)
    act_other = swap(act, "group", 1)
    rounds = [("ingroup", 1), ("ingroup", 2), ("group", 1)]
    bit = n_hid // 2
    while bit:
        rounds.append(("hid", bit))
        bit //= 2
    weights = [1] * (len(rounds) - 1)
    pieces = [[]] + cut(own, n_group, weights)
    out, mark = None, scal
    for (axis, bit), piece in zip(rounds, pieces):
        got = swap(send, axis, bit)
        for part in piece:
            *out, mark = grads(scal, act if part[0] == 0 else act_other, xs, gs, part, out, mark, grad_shape, n_group, slots)
        if axis == "ingroup" and bit == 2:
            keep, got = keep[0], got[0]
        keep, *rest = add_halves(keep, got, mark)
        mark = keep
        send = rest[0] if rest else None
    return (keep[0, 0], keep[0, 1], jnp.swapaxes(out[0], 1, 2), jnp.swapaxes(out[1], 1, 2), out[2])


def cut(own, n_group, weights):
    total = own * n_group
    ends = [total * sum(weights[:k + 1]) // sum(weights) for k in range(len(weights))]
    pieces, at = [], 0
    for end in ends:
        piece = []
        while at < end:
            which, first = divmod(at, own)
            count = min(end - at, own - first)
            piece.append((which, first, count))
            at += count
        pieces.append(piece)
    return pieces


def solution(mesh):
    placed = (
        P(("group", "hid"), None),
        P(("group", "hid"), None),
        P(("group", "hid"), None),
        P(("group", "hid"), None),
        P("hid", None, "ingroup"),
        P("hid", None, "ingroup"),
        P("hid", "ingroup", None),
    )
    return jax.shard_map(
        shards,
        mesh=mesh,
        in_specs=placed,
        out_specs=(
            P(("group", "hid"), "ingroup"),
            P(("group", "hid"), "ingroup"),
            P("hid", "group", "ingroup"),
            P("hid", "group", "ingroup"),
            P("hid", "ingroup", "group"),
        ),
        check_vma=False,
    )
```

```python
import functools

import jax
import jax.numpy as jnp
from jax import lax
from jax.experimental import pallas as pl
from jax.experimental.pallas import tpu as pltpu
from jax.sharding import PartitionSpec as P

TOP = 6


def plain(tokens, grad_mixed, expert_ids, gate_weight, w_gate, w_up, w_down):
    tok_count = tokens.shape[0]
    width = tokens.shape[1]
    n_hid = lax.axis_size("hid")
    exp_dev = w_gate.shape[0]
    experts_all = exp_dev * n_hid
    capacity = tok_count // 8
    slots_total = experts_all * capacity
    flat = expert_ids.reshape(tok_count * TOP)
    onehot = (flat[:, None] == jnp.arange(experts_all, dtype=jnp.int32)[None, :]).astype(jnp.int32)
    rank = jnp.sum((jnp.cumsum(onehot, axis=0) - onehot) * onehot, axis=1)
    owner_idx = flat // exp_dev
    local_idx = flat % exp_dev
    slot = (local_idx * n_hid + owner_idx) * capacity + rank
    token_index = jnp.arange(tok_count * TOP, dtype=jnp.int32) // TOP
    token_of = jnp.zeros((slots_total,), jnp.int32).at[slot].set(token_index)
    live_of = jnp.zeros((slots_total,), jnp.bool_).at[slot].set(True)
    gate_of = (
        jnp.zeros((slots_total,), jnp.float32).at[slot].set(gate_weight.reshape(tok_count * TOP))
    )
    send_x = jnp.where(live_of[:, None], tokens[token_of], jnp.zeros((), jnp.bfloat16))
    send_g = (gate_of[:, None] * grad_mixed[token_of].astype(jnp.float32)).astype(jnp.bfloat16)
    shape_whole = (exp_dev, n_hid, capacity, width)
    recv_x, recv_g = (
        lax.all_to_all(send_x.reshape(shape_whole), "hid", split_axis=1, concat_axis=1, tiled=True),
        lax.all_to_all(send_g.reshape(shape_whole), "hid", split_axis=1, concat_axis=1, tiled=True),
    )
    rows = n_hid * capacity
    x_rows = recv_x.reshape(exp_dev, rows, width)
    gated = recv_g.reshape(exp_dev, rows, width)
    gate_pre = jnp.einsum("emd,edh->emh", x_rows, w_gate, preferred_element_type=jnp.float32)
    up_pre = jnp.einsum("emd,edh->emh", x_rows, w_up, preferred_element_type=jnp.float32)
    sigmoid_gate = jax.nn.sigmoid(gate_pre)
    silu = gate_pre * sigmoid_gate
    hidden = (silu * up_pre).astype(jnp.bfloat16)
    out_part = jnp.einsum("emh,ehd->emd", hidden, w_down, preferred_element_type=jnp.float32)
    d_hidden = jnp.einsum("emd,ehd->emh", gated, w_down, preferred_element_type=jnp.float32)
    d_up = (d_hidden * silu).astype(jnp.bfloat16)
    d_gate = (d_hidden * up_pre * sigmoid_gate * (1.0 + gate_pre * (1.0 - sigmoid_gate))).astype(
        jnp.bfloat16
    )
    term_down = jnp.einsum("emh,emd->ehd", hidden, gated, preferred_element_type=jnp.float32)
    term_gate = jnp.einsum("emd,emh->edh", x_rows, d_gate, preferred_element_type=jnp.float32)
    term_up = jnp.einsum("emd,emh->edh", x_rows, d_up, preferred_element_type=jnp.float32)
    in_part = jnp.einsum("emh,edh->emd", d_gate, w_gate, preferred_element_type=jnp.float32)
    in_part = in_part + jnp.einsum("emh,edh->emd", d_up, w_up, preferred_element_type=jnp.float32)
    grad_gate, grad_up, grad_down = (
        lax.psum_scatter(
            term_gate.astype(jnp.bfloat16), "group", scatter_dimension=1, tiled=True
        ).astype(jnp.float32),
        lax.psum_scatter(
            term_up.astype(jnp.bfloat16), "group", scatter_dimension=1, tiled=True
        ).astype(jnp.float32),
        lax.psum_scatter(
            term_down.astype(jnp.bfloat16), "group", scatter_dimension=2, tiled=True
        ).astype(jnp.float32),
    )
    out_share, in_share = (
        lax.psum_scatter(
            out_part.astype(jnp.bfloat16), "ingroup", scatter_dimension=2, tiled=True
        ).astype(jnp.float32),
        lax.psum_scatter(
            in_part.astype(jnp.bfloat16), "ingroup", scatter_dimension=2, tiled=True
        ).astype(jnp.float32),
    )
    narrow = out_share.shape[2]
    out_share = out_share.astype(jnp.bfloat16)
    in_share = in_share.astype(jnp.bfloat16)
    back_shape = (exp_dev, n_hid, capacity, narrow)
    home_out, home_in = (
        lax.all_to_all(
            out_share.reshape(back_shape), "hid", split_axis=1, concat_axis=1, tiled=True
        ),
        lax.all_to_all(
            in_share.reshape(back_shape), "hid", split_axis=1, concat_axis=1, tiled=True
        ),
    )
    picked_out = home_out.reshape(slots_total, narrow)[slot].reshape(tok_count, TOP, narrow)
    picked_in = home_in.reshape(slots_total, narrow)[slot].reshape(tok_count, TOP, narrow)
    mixed = jnp.sum(gate_weight[:, :, None] * picked_out.astype(jnp.float32), axis=1).astype(
        jnp.bfloat16
    )
    grad_tokens = jnp.sum(picked_in.astype(jnp.float32), axis=1).astype(jnp.bfloat16)
    return (mixed, grad_tokens, grad_gate, grad_up, grad_down)


def middle_kernel(sizes, places, scal, wg_ref, wu_ref, wd_ref, *refs):
    n_group, n_ingroup, n_hid, tok, experts, half, cap = sizes
    message_refs, refs = refs[:2 * len(places)], refs[2 * len(places):]
    keep_ref, send_ref, act_ref, xs_ref, gs_ref = refs[:5]
    x_scr, g_scr, c_scr, w_scr, pick_scr, wbuf, val_scr, acc_o, acc_i, sem = refs[5:]
    ff, width = act_ref.shape[2], wbuf.shape[2]
    exp_own = wbuf.shape[1] // ff
    rows = n_group * n_hid * tok
    wide = width // 2
    g, i, h = scal[0], scal[1], scal[2]
    core = lax.rem(i, 2)
    base = g * exp_own
    pair = 4

    def fetch(e, k, ref):
        return pltpu.make_async_copy(ref.at[base + e], wbuf.at[k, pl.ds(pl.multiple_of(e * ff, ff), ff)], sem.at[k, e])

    for e0 in range(0, exp_own, pair):
        for k, ref in enumerate((wg_ref, wu_ref, wd_ref)):
            for e in range(pair):
                fetch(e0 + e, k, ref).start()

    for m, place in enumerate(places):
        for ref, part in ((message_refs[2 * m], core), (message_refs[2 * m + 1], 1 - core)):
            for at_msg, (s, d) in enumerate(place):
                block = lax.rem(g + s, n_group) * n_hid + lax.rem(h - d + n_hid, n_hid)
                at = pl.ds(pl.multiple_of(block * tok, tok), tok)
                cols = pl.ds(pl.multiple_of(part * wide, wide), wide)
                x_scr[at, cols] = ref[at_msg, :, :wide]
                g_scr[at, cols] = ref[at_msg, :, wide:2 * wide]
                c_scr[part, at, :] = ref[at_msg, :, 2 * wide:].astype(jnp.float32)

    lanes = c_scr.shape[2]
    first, second = c_scr[0], c_scr[1]
    weight = first + pltpu.roll(first, lanes - experts, 1) + second
    lane = lax.broadcasted_iota(jnp.int32, (rows, lanes), 1)
    weight = jnp.where(lane < experts, weight, 0.0)
    w_scr[...] = weight
    routed = (weight > 0).astype(jnp.bfloat16)
    row_a = lax.broadcasted_iota(jnp.int32, (rows, rows), 0)
    row_b = lax.broadcasted_iota(jnp.int32, (rows, rows), 1)
    before = ((row_a // tok == row_b // tok) & (row_b < row_a)).astype(jnp.bfloat16)
    rank = jnp.dot(before, routed, preferred_element_type=jnp.float32)
    block_of = (lax.broadcasted_iota(jnp.int32, (rows, lanes), 0) // tok).astype(jnp.float32)
    slot = jnp.where(weight > 0, rank + cap * block_of, -1.0)
    slots = n_group * n_hid * cap
    spread_e = lax.broadcasted_iota(jnp.int32, (lanes, exp_own * slots), 0)
    spread_l = lax.broadcasted_iota(jnp.int32, (lanes, exp_own * slots), 1)
    lane_s = lax.broadcasted_iota(jnp.int32, (rows, exp_own * slots), 1)
    for which in range(n_group):
        owner = h * (exp_own * n_group) + lax.rem(g + which, n_group) * exp_own
        spread = (spread_e == owner + spread_l // slots).astype(jnp.bfloat16)
        slot_l = jnp.dot(slot.astype(jnp.bfloat16), spread, preferred_element_type=jnp.float32)
        pick = (slot_l == (lane_s % slots).astype(jnp.float32)).astype(jnp.float32).T.astype(jnp.bfloat16)
        if which == 0:
            pick_scr[...] = pick
        xs_ref[which] = jnp.dot(pick, x_scr[:, pl.ds(pl.multiple_of(g * wide, wide), wide)],
                                preferred_element_type=jnp.float32).astype(jnp.bfloat16)
        gs_ref[which] = jnp.dot(pick, g_scr[:, pl.ds(pl.multiple_of(g * wide, wide), wide)],
                                preferred_element_type=jnp.float32).astype(jnp.bfloat16)

    nt = (((1,), (1,)), ((), ()))
    lane_f = lax.broadcasted_iota(jnp.int32, (rows, pair * ff), 1)

    def step(j, carry):
        e0 = j * pair
        w_at = pl.ds(pl.multiple_of(e0 * ff, pair * ff), pair * ff)
        pre = []
        for k, (ref, rows_of) in enumerate(((wg_ref, x_scr), (wu_ref, x_scr), (wd_ref, g_scr))):
            for e in range(pair):
                fetch(e0 + e, k, ref).wait()
            pre.append(lax.dot_general(rows_of[...], wbuf[k, w_at, :], nt, preferred_element_type=jnp.float32))
        gate, up, back = pre
        at = h * (exp_own * n_group) + base + e0
        col = [jnp.sum(jnp.where(lane == at + e, w_scr[...], 0.0), axis=1, keepdims=True) for e in range(pair)]
        scale = col[0]
        for e in range(1, pair):
            scale = jnp.where(lane_f < e * ff, scale, col[e])
        sig = jax.nn.sigmoid(gate)
        silu = gate * sig
        d_hid = back * scale
        hid = (silu * up * scale).astype(jnp.bfloat16)
        d_up = (d_hid * silu).astype(jnp.bfloat16)
        d_gate = (d_hid * up * sig * (1.0 + gate * (1.0 - sig))).astype(jnp.bfloat16)
        pick = pick_scr[pl.ds(pl.multiple_of(e0 * slots, pair * slots), pair * slots), :]
        for k, val in enumerate((d_gate, d_up, hid)):
            packed = jnp.dot(pick, val, preferred_element_type=jnp.float32).astype(jnp.bfloat16)
            for e in range(pair):
                act_ref[k, pl.ds(pl.multiple_of((e0 + e) * slots, slots), slots), :] = packed[
                    e * slots:(e + 1) * slots, e * ff:(e + 1) * ff]
        for k, val in enumerate((d_gate, d_up, hid)):
            val_scr[k, :, w_at] = val
        return carry

    lax.fori_loop(0, exp_own // pair, step, 0)
    acc_o[...] = jnp.dot(val_scr[2], wbuf[2], preferred_element_type=jnp.float32)
    acc_i[...] = (jnp.dot(val_scr[0], wbuf[0], preferred_element_type=jnp.float32)
                  + jnp.dot(val_scr[1], wbuf[1], preferred_element_type=jnp.float32))
    narrow = width // n_ingroup
    for y in range(2):
        for b in range(n_group * n_hid):
            rel = (y ^ (i // 2)) * (n_group * n_hid) + (b ^ (g * n_hid + h))
            at = slice(b * tok, (b + 1) * tok)
            for k, acc in enumerate((acc_o, acc_i)):
                two = [acc[at, (2 * y + c) * narrow:(2 * y + c + 1) * narrow].astype(jnp.bfloat16) for c in range(2)]
                keep_ref[rel, k] = jnp.where(core == 0, two[0], two[1])
                send_ref[rel, k] = jnp.where(core == 0, two[1], two[0])


def add_kernel(keep_ref, got_ref, mark_ref, *out_refs):
    del mark_ref
    size = keep_ref.shape[0] // 2
    for k, out in enumerate(out_refs):
        at = slice(k * size, (k + 1) * size) if size else (0, k)
        out[...] = (keep_ref[at].astype(jnp.float32) + got_ref[at].astype(jnp.float32)).astype(out.dtype)


def add_halves(keep, got, mark):
    vmem = pl.BlockSpec(memory_space=pltpu.VMEM)
    shape = (keep.shape[0] // 2,) + keep.shape[1:] if keep.shape[0] > 1 else keep.shape[2:]
    return pl.pallas_call(
        add_kernel,
        out_shape=[jax.ShapeDtypeStruct(shape, keep.dtype)] * 2,
        in_specs=[vmem, vmem, pl.BlockSpec(memory_space=pl.ANY)],
        out_specs=[vmem] * 2,
        compiler_params=pltpu.CompilerParams(vmem_limit_bytes=4 << 20),
        cost_estimate=pl.CostEstimate(flops=keep.size, bytes_accessed=keep.size * 6, transcendentals=0),
        name="add_halves",
    )(keep, got, mark)


def grad_kernel(piece, slots, n_group, scal, act_ref, xs_ref, gs_ref, *refs):
    which, first, count = piece
    *outs, mark_ref, stage, sem = refs[-6:]
    mark_ref[...] = jnp.zeros_like(mark_ref)
    own = act_ref.shape[1] // slots
    base = lax.rem(scal[0] + which, n_group) * own + first
    tn = (((0,), (0,)), ((), ()))
    depth = stage.shape[0]

    def put(j, k):
        slot = lax.rem(j, depth)
        return pltpu.make_async_copy(stage.at[slot, k], outs[k].at[base + j], sem.at[slot, k])

    def step(j, carry):
        at = pl.ds(pl.multiple_of((first + j) * slots, slots), slots)
        for k, right in enumerate((xs_ref, xs_ref, gs_ref)):
            @pl.when(j >= depth)
            def _():
                put(j - depth, k).wait()
            stage[lax.rem(j, depth), k] = lax.dot_general(
                act_ref[k, at, :], right[which, at, :], tn, preferred_element_type=jnp.float32)
            put(j, k).start()
        return carry

    lax.fori_loop(0, count, step, 0)
    for j in range(max(0, count - depth), count):
        for k in range(3):
            put(j, k).wait()


def grads(scal, act, xs, gs, piece, out, after, shape, n_group, slots):
    ff, wide, count = act.shape[2], xs.shape[2], piece[2]
    depth = min(2, count)
    vmem, any_space = pl.BlockSpec(memory_space=pltpu.VMEM), pl.BlockSpec(memory_space=pl.ANY)
    return pl.pallas_call(
        functools.partial(grad_kernel, piece, slots, n_group),
        out_shape=[shape] * 3 + [jax.ShapeDtypeStruct((8, 128), jnp.float32)],
        in_specs=[pl.BlockSpec(memory_space=pltpu.SMEM)] + [vmem] * 3 + [any_space] * (4 if out else 1),
        out_specs=[any_space] * 3 + [vmem],
        scratch_shapes=[pltpu.VMEM((depth, 3, ff, wide), jnp.float32), pltpu.SemaphoreType.DMA((depth, 3))],
        input_output_aliases={5 + k: k for k in range(3)} if out else {},
        compiler_params=pltpu.CompilerParams(vmem_limit_bytes=12 << 20),
        cost_estimate=pl.CostEstimate(
            flops=count * 3 * 2 * ff * slots * wide,
            bytes_accessed=count * 3 * ff * wide * 4, transcendentals=0),
        name="weight_grads",
    )(scal, act, xs, gs, after, *(out or ()))


def swap(x, axis, bit):
    n = lax.axis_size(axis)
    return lax.ppermute(x, axis, [(k, k ^ bit) for k in range(n)])


def shards(tokens, grad_mixed, expert_ids, gate_weight, w_gate, w_up, w_down):
    tok, width = tokens.shape
    n_group, n_ingroup, n_hid = (lax.axis_size(a) for a in ("group", "ingroup", "hid"))
    exp_dev, ff = w_down.shape[0], w_down.shape[1]
    experts = exp_dev * n_hid
    cap = tok // 8
    own = exp_dev // n_group
    rows = n_group * n_hid * tok
    slots = n_group * n_hid * cap
    if not (n_group == 2 and n_ingroup == 4 and exp_dev % (2 * n_group) == 0 and n_hid & (n_hid - 1) == 0
            and rows == 128 and own * slots == 128 and 2 * experts <= 128):
        return plain(tokens, grad_mixed, expert_ids, gate_weight, w_gate, w_up, w_down)
    g, i, h = (lax.axis_index(a) for a in ("group", "ingroup", "hid"))
    scal = jnp.stack([g, i, h]).astype(jnp.int32)
    core = lax.rem(i, 2)
    half = width // 2
    table = jnp.sum(jnp.where(expert_ids[:, :, None] == jnp.arange(experts, dtype=jnp.int32)[None, None, :],
                              gate_weight[:, :, None], 0.0), axis=1)
    hi = lax.reduce_precision(table, 8, 7)
    mid = lax.reduce_precision(table - hi, 8, 7)
    low = lax.reduce_precision(table - hi - mid, 8, 7)
    zero = jnp.zeros_like(hi)
    terms = jnp.where(core == 0, jnp.concatenate([hi, mid], 1), jnp.concatenate([low, zero], 1))
    message = jnp.concatenate([
        lax.dynamic_slice_in_dim(tokens, core * half, half, 1),
        lax.dynamic_slice_in_dim(grad_mixed, core * half, half, 1),
        terms.astype(jnp.bfloat16)], axis=1)
    line = [message] + [lax.ppermute(message, "hid", [(k, (k + d) % n_hid) for k in range(n_hid)])
                        for d in range(1, n_hid)]
    messages, places = [], []
    for low in range(0, n_hid, n_hid // 2):
        group_of = range(low, low + n_hid // 2)
        mine = jnp.stack([line[d] for d in group_of])
        for s, block in enumerate((mine, swap(mine, "group", 1))):
            messages += [block, swap(block, "ingroup", 1)]
            places.append(tuple((s, d) for d in group_of))
    wg, wu = jnp.swapaxes(w_gate, 1, 2), jnp.swapaxes(w_up, 1, 2)
    narrow = width // n_ingroup
    any_space = pl.BlockSpec(memory_space=pl.ANY)
    vmem = pl.BlockSpec(memory_space=pltpu.VMEM)
    lanes = message.shape[1] - 2 * half
    keep, send, act, xs, gs = pl.pallas_call(
        functools.partial(middle_kernel, (n_group, n_ingroup, n_hid, tok, experts, half, cap), tuple(places)),
        out_shape=[
            jax.ShapeDtypeStruct((n_group * n_hid * 2, 2, tok, narrow), jnp.bfloat16),
            jax.ShapeDtypeStruct((n_group * n_hid * 2, 2, tok, narrow), jnp.bfloat16),
            jax.ShapeDtypeStruct((3, own * slots, ff), jnp.bfloat16),
            jax.ShapeDtypeStruct((n_group, own * slots, half), jnp.bfloat16),
            jax.ShapeDtypeStruct((n_group, own * slots, half), jnp.bfloat16),
        ],
        in_specs=[pl.BlockSpec(memory_space=pltpu.SMEM)] + [any_space] * 3 + [vmem] * len(messages),
        out_specs=[vmem] * 5,
        scratch_shapes=[
            pltpu.VMEM((rows, width), jnp.bfloat16),
            pltpu.VMEM((rows, width), jnp.bfloat16),
            pltpu.VMEM((2, rows, lanes), jnp.float32),
            pltpu.VMEM((rows, lanes), jnp.float32),
            pltpu.VMEM((own * slots, rows), jnp.bfloat16),
            pltpu.VMEM((3, own * ff, width), jnp.bfloat16),
            pltpu.VMEM((3, rows, own * ff), jnp.bfloat16),
            pltpu.VMEM((rows, width), jnp.float32),
            pltpu.VMEM((rows, width), jnp.float32),
            pltpu.SemaphoreType.DMA((3, own)),
        ],
        compiler_params=pltpu.CompilerParams(vmem_limit_bytes=48 << 20),
        cost_estimate=pl.CostEstimate(flops=6 * 2 * own * ff * width * rows,
                                      bytes_accessed=3 * own * ff * width * 2, transcendentals=own * ff * rows),
        name="experts",
    )(scal, wg, wu, w_down, *messages)
    grad_shape = jax.ShapeDtypeStruct((exp_dev, ff, width // n_group), jnp.float32)
    act_other = swap(act, "group", 1)
    rounds = [("ingroup", 1), ("ingroup", 2), ("group", 1)]
    bit = n_hid // 2
    while bit:
        rounds.append(("hid", bit))
        bit //= 2
    pieces = cut(own, n_group, [0] + [1] * (len(rounds) - 1))
    out, mark = None, scal
    for (axis, bit), piece in zip(rounds, pieces):
        got = swap(send, axis, bit)
        for part in piece:
            *out, mark = grads(scal, act if part[0] == 0 else act_other, xs, gs, part, out, mark, grad_shape, n_group, slots)
        keep, send = add_halves(keep, got, mark)
        mark = keep
    return (keep, send, jnp.swapaxes(out[0], 1, 2), jnp.swapaxes(out[1], 1, 2), out[2])


def cut(own, n_group, weights):
    total = own * n_group
    ends = [total * sum(weights[:k + 1]) // sum(weights) for k in range(len(weights))]
    pieces, at = [], 0
    for end in ends:
        piece = []
        while at < end:
            which, first = divmod(at, own)
            count = min(end - at, own - first)
            piece.append((which, first, count))
            at += count
        pieces.append(piece)
    return pieces


def solution(mesh):
    placed = (
        P(("group", "hid"), None),
        P(("group", "hid"), None),
        P(("group", "hid"), None),
        P(("group", "hid"), None),
        P("hid", None, "ingroup"),
        P("hid", None, "ingroup"),
        P("hid", "ingroup", None),
    )
    return jax.shard_map(
        shards,
        mesh=mesh,
        in_specs=placed,
        out_specs=(
            P(("group", "hid"), "ingroup"),
            P(("group", "hid"), "ingroup"),
            P("hid", "group", "ingroup"),
            P("hid", "group", "ingroup"),
            P("hid", "ingroup", "group"),
        ),
        check_vma=False,
    )
```

```python
import functools

import jax
import jax.numpy as jnp
from jax import lax
from jax.experimental import pallas as pl
from jax.experimental.pallas import tpu as pltpu
from jax.sharding import PartitionSpec as P


TOP = 6


def plain(tokens, grad_mixed, expert_ids, gate_weight, w_gate, w_up, w_down):
    tok_count = tokens.shape[0]
    width = tokens.shape[1]
    n_hid = lax.axis_size("hid")
    exp_dev = w_gate.shape[0]
    experts_all = exp_dev * n_hid
    capacity = tok_count // 8
    slots_total = experts_all * capacity
    flat = expert_ids.reshape(tok_count * TOP)
    onehot = (flat[:, None] == jnp.arange(experts_all, dtype=jnp.int32)[None, :]).astype(jnp.int32)
    rank = jnp.sum((jnp.cumsum(onehot, axis=0) - onehot) * onehot, axis=1)
    owner_idx = flat // exp_dev
    local_idx = flat % exp_dev
    slot = (local_idx * n_hid + owner_idx) * capacity + rank
    token_index = jnp.arange(tok_count * TOP, dtype=jnp.int32) // TOP
    token_of = jnp.zeros((slots_total,), jnp.int32).at[slot].set(token_index)
    live_of = jnp.zeros((slots_total,), jnp.bool_).at[slot].set(True)
    gate_of = (
        jnp.zeros((slots_total,), jnp.float32).at[slot].set(gate_weight.reshape(tok_count * TOP))
    )
    send_x = jnp.where(live_of[:, None], tokens[token_of], jnp.zeros((), jnp.bfloat16))
    send_g = (gate_of[:, None] * grad_mixed[token_of].astype(jnp.float32)).astype(jnp.bfloat16)
    shape_whole = (exp_dev, n_hid, capacity, width)
    recv_x, recv_g = (
        lax.all_to_all(send_x.reshape(shape_whole), "hid", split_axis=1, concat_axis=1, tiled=True),
        lax.all_to_all(send_g.reshape(shape_whole), "hid", split_axis=1, concat_axis=1, tiled=True),
    )
    rows = n_hid * capacity
    x_rows = recv_x.reshape(exp_dev, rows, width)
    gated = recv_g.reshape(exp_dev, rows, width)
    gate_pre = jnp.einsum("emd,edh->emh", x_rows, w_gate, preferred_element_type=jnp.float32)
    up_pre = jnp.einsum("emd,edh->emh", x_rows, w_up, preferred_element_type=jnp.float32)
    sigmoid_gate = jax.nn.sigmoid(gate_pre)
    silu = gate_pre * sigmoid_gate
    hidden = (silu * up_pre).astype(jnp.bfloat16)
    out_part = jnp.einsum("emh,ehd->emd", hidden, w_down, preferred_element_type=jnp.float32)
    d_hidden = jnp.einsum("emd,ehd->emh", gated, w_down, preferred_element_type=jnp.float32)
    d_up = (d_hidden * silu).astype(jnp.bfloat16)
    d_gate = (d_hidden * up_pre * sigmoid_gate * (1.0 + gate_pre * (1.0 - sigmoid_gate))).astype(
        jnp.bfloat16
    )
    term_down = jnp.einsum("emh,emd->ehd", hidden, gated, preferred_element_type=jnp.float32)
    term_gate = jnp.einsum("emd,emh->edh", x_rows, d_gate, preferred_element_type=jnp.float32)
    term_up = jnp.einsum("emd,emh->edh", x_rows, d_up, preferred_element_type=jnp.float32)
    in_part = jnp.einsum("emh,edh->emd", d_gate, w_gate, preferred_element_type=jnp.float32)
    in_part = in_part + jnp.einsum("emh,edh->emd", d_up, w_up, preferred_element_type=jnp.float32)
    grad_gate, grad_up, grad_down = (
        lax.psum_scatter(
            term_gate.astype(jnp.bfloat16), "group", scatter_dimension=1, tiled=True
        ).astype(jnp.float32),
        lax.psum_scatter(
            term_up.astype(jnp.bfloat16), "group", scatter_dimension=1, tiled=True
        ).astype(jnp.float32),
        lax.psum_scatter(
            term_down.astype(jnp.bfloat16), "group", scatter_dimension=2, tiled=True
        ).astype(jnp.float32),
    )
    out_share, in_share = (
        lax.psum_scatter(
            out_part.astype(jnp.bfloat16), "ingroup", scatter_dimension=2, tiled=True
        ).astype(jnp.float32),
        lax.psum_scatter(
            in_part.astype(jnp.bfloat16), "ingroup", scatter_dimension=2, tiled=True
        ).astype(jnp.float32),
    )
    narrow = out_share.shape[2]
    out_share = out_share.astype(jnp.bfloat16)
    in_share = in_share.astype(jnp.bfloat16)
    back_shape = (exp_dev, n_hid, capacity, narrow)
    home_out, home_in = (
        lax.all_to_all(
            out_share.reshape(back_shape), "hid", split_axis=1, concat_axis=1, tiled=True
        ),
        lax.all_to_all(
            in_share.reshape(back_shape), "hid", split_axis=1, concat_axis=1, tiled=True
        ),
    )
    picked_out = home_out.reshape(slots_total, narrow)[slot].reshape(tok_count, TOP, narrow)
    picked_in = home_in.reshape(slots_total, narrow)[slot].reshape(tok_count, TOP, narrow)
    mixed = jnp.sum(gate_weight[:, :, None] * picked_out.astype(jnp.float32), axis=1).astype(
        jnp.bfloat16
    )
    grad_tokens = jnp.sum(picked_in.astype(jnp.float32), axis=1).astype(jnp.bfloat16)
    return (mixed, grad_tokens, grad_gate, grad_up, grad_down)


def prefetch_kernel(exp_own, scal, after, w_ref, out_ref, sem):
    del after
    ff = w_ref.shape[1]
    copies = [pltpu.make_async_copy(w_ref.at[scal[0] * exp_own + e], out_ref.at[pl.ds(e * ff, ff)], sem.at[e])
              for e in range(sem.shape[0])]
    for copy in copies:
        copy.start()
    for copy in copies:
        copy.wait()


def middle_kernel(sizes, places, scal, w0_ref, wg_ref, wu_ref, wd_ref, *refs):
    n_group, n_ingroup, n_hid, tok, experts, _, cap = sizes
    message_refs, refs = refs[:2 * len(places)], refs[2 * len(places):]
    keep_ref, send_ref, act_ref, xs_ref, gs_ref = refs[:5]
    x_scr, g_scr, c_scr, w_scr, pick_scr, wbuf, val_scr, acc_o, acc_i, sem = refs[5:]
    ff, width = act_ref.shape[2], wbuf.shape[1]
    exp_own = (wbuf.shape[0] + w0_ref.shape[0]) // (3 * ff)
    rows = n_group * n_hid * tok
    wide = width // 2
    g, i, h = scal[0], scal[1], scal[2]
    core = lax.rem(i, 2)
    base = g * exp_own
    pair = 4

    def row(k, e):
        return (k * exp_own + e) * ff - w0_ref.shape[0]

    def fetch(e, k, ref):
        return pltpu.make_async_copy(ref.at[base + e], wbuf.at[pl.ds(row(k, e), ff)], sem.at[k, e])

    for e0 in range(0, exp_own, pair):
        for k, ref in enumerate((wg_ref, wu_ref, wd_ref)):
            for e in range(pair if e0 + k > 0 else 0):
                fetch(e0 + e, k, ref).start()

    for m, place in enumerate(places):
        for ref, part in ((message_refs[2 * m], core), (message_refs[2 * m + 1], 1 - core)):
            for at_msg, (s, d) in enumerate(place):
                block = lax.rem(g + s, n_group) * n_hid + lax.rem(h - d + n_hid, n_hid)
                at = pl.ds(pl.multiple_of(block * tok, tok), tok)
                cols = pl.ds(pl.multiple_of(part * wide, wide), wide)
                x_scr[at, cols] = ref[at_msg, :, :wide]
                g_scr[at, cols] = ref[at_msg, :, wide:2 * wide]
                c_scr[part, at, :] = ref[at_msg, :, 2 * wide:].astype(jnp.float32)

    lanes = c_scr.shape[2]
    first, second = c_scr[0], c_scr[1]
    weight = first + pltpu.roll(first, lanes - experts, 1) + second
    lane = lax.broadcasted_iota(jnp.int32, (rows, lanes), 1)
    weight = jnp.where(lane < experts, weight, 0.0)
    w_scr[...] = weight
    routed = (weight > 0).astype(jnp.bfloat16)
    row_a = lax.broadcasted_iota(jnp.int32, (rows, rows), 0)
    row_b = lax.broadcasted_iota(jnp.int32, (rows, rows), 1)
    before = ((row_a // tok == row_b // tok) & (row_b < row_a)).astype(jnp.bfloat16)
    rank = jnp.dot(before, routed, preferred_element_type=jnp.float32)
    block_of = (lax.broadcasted_iota(jnp.int32, (rows, lanes), 0) // tok).astype(jnp.float32)
    slot = jnp.where(weight > 0, rank + cap * block_of, -1.0)
    slots = n_group * n_hid * cap
    spread_e = lax.broadcasted_iota(jnp.int32, (lanes, exp_own * slots), 0)
    spread_l = lax.broadcasted_iota(jnp.int32, (lanes, exp_own * slots), 1)
    lane_s = lax.broadcasted_iota(jnp.int32, (rows, exp_own * slots), 1)
    for which in range(n_group):
        owner = h * (exp_own * n_group) + lax.rem(g + which, n_group) * exp_own
        spread = (spread_e == owner + spread_l // slots).astype(jnp.bfloat16)
        slot_l = jnp.dot(slot.astype(jnp.bfloat16), spread, preferred_element_type=jnp.float32)
        pick = (slot_l == (lane_s % slots).astype(jnp.float32)).astype(jnp.float32).T.astype(jnp.bfloat16)
        if which == 0:
            pick_scr[...] = pick
        xs_ref[which] = jnp.dot(pick, x_scr[:, pl.ds(pl.multiple_of(g * wide, wide), wide)],
                                preferred_element_type=jnp.float32).astype(jnp.bfloat16)
        gs_ref[which] = jnp.dot(pick, g_scr[:, pl.ds(pl.multiple_of(g * wide, wide), wide)],
                                preferred_element_type=jnp.float32).astype(jnp.bfloat16)

    nt = (((1,), (1,)), ((), ()))
    lane_f = lax.broadcasted_iota(jnp.int32, (rows, pair * ff), 1)

    for j in range(exp_own // pair):
        e0 = j * pair
        w_at = slice(e0 * ff, (e0 + pair) * ff)
        pre = []
        for k, (ref, rows_of) in enumerate(((wg_ref, x_scr), (wu_ref, x_scr), (wd_ref, g_scr))):
            for e in range(pair if e0 + k > 0 else 0):
                fetch(e0 + e, k, ref).wait()
            pre.append(lax.dot_general(rows_of[...], wbuf[row(k, e0):row(k, e0 + pair), :] if e0 + k > 0 else w0_ref[...], nt, preferred_element_type=jnp.float32))
        gate, up, back = pre
        at = h * (exp_own * n_group) + base + e0
        col = [jnp.sum(jnp.where(lane == at + e, w_scr[...], 0.0), axis=1, keepdims=True) for e in range(pair)]
        scale = col[0]
        for e in range(1, pair):
            scale = jnp.where(lane_f < e * ff, scale, col[e])
        sig = 0.5 + 0.5 * jnp.tanh(0.5 * gate)
        silu = gate * sig
        d_hid = back * scale
        hid = (silu * up * scale).astype(jnp.bfloat16)
        d_up = (d_hid * silu).astype(jnp.bfloat16)
        d_gate = (d_hid * up * (sig + silu * (1.0 - sig))).astype(jnp.bfloat16)
        pick = pick_scr[e0 * slots:(e0 + pair) * slots, :]
        for k, val in enumerate((d_gate, d_up, hid)):
            packed = jnp.dot(pick, val, preferred_element_type=jnp.float32).astype(jnp.bfloat16)
            for e in range(pair):
                act_ref[k, (e0 + e) * slots:(e0 + e + 1) * slots, :] = packed[
                    e * slots:(e + 1) * slots, e * ff:(e + 1) * ff]
        for k, val in enumerate((d_gate, d_up, hid)):
            val_scr[k, :, w_at] = val

    cut_at = pair * ff
    acc_o[...] = jnp.dot(val_scr[2], wbuf[row(2, 0):row(3, 0), :], preferred_element_type=jnp.float32)
    acc_i[...] = (jnp.dot(val_scr[0, :, :cut_at], w0_ref[...], preferred_element_type=jnp.float32)
                  + jnp.dot(val_scr[0, :, cut_at:], wbuf[row(0, pair):row(1, 0), :], preferred_element_type=jnp.float32)
                  + jnp.dot(val_scr[1], wbuf[row(1, 0):row(2, 0), :], preferred_element_type=jnp.float32))
    narrow = width // n_ingroup
    for y in range(2):
        for b in range(n_group * n_hid):
            rel = (y ^ (i // 2)) * (n_group * n_hid) + (b ^ (g * n_hid + h))
            at = slice(b * tok, (b + 1) * tok)
            for k, acc in enumerate((acc_o, acc_i)):
                two = [acc[at, (2 * y + c) * narrow:(2 * y + c + 1) * narrow].astype(jnp.bfloat16) for c in range(2)]
                keep_ref[rel, k] = jnp.where(core == 0, two[0], two[1])
                send_ref[rel, k] = jnp.where(core == 0, two[1], two[0])


def add_kernel(keep_ref, got_ref, mark_ref, *out_refs):
    del mark_ref
    size = keep_ref.shape[0] // 2
    for k, out in enumerate(out_refs):
        at = slice(k * size, (k + 1) * size) if size else (0, k)
        out[...] = (keep_ref[at].astype(jnp.float32) + got_ref[at].astype(jnp.float32)).astype(out.dtype)


def add_halves(keep, got, mark):
    vmem = pl.BlockSpec(memory_space=pltpu.VMEM)
    shape = (keep.shape[0] // 2,) + keep.shape[1:] if keep.shape[0] > 1 else keep.shape[2:]
    return pl.pallas_call(
        add_kernel,
        out_shape=[jax.ShapeDtypeStruct(shape, keep.dtype)] * 2,
        in_specs=[vmem, vmem, pl.BlockSpec(memory_space=pl.ANY)],
        out_specs=[vmem] * 2,
        compiler_params=pltpu.CompilerParams(vmem_limit_bytes=4 << 20),
        cost_estimate=pl.CostEstimate(flops=keep.size, bytes_accessed=keep.size * 6, transcendentals=0),
        name="add_halves",
    )(keep, got, mark)


def grad_kernel(piece, slots, n_group, scal, act_ref, xs_ref, gs_ref, *refs):
    which, first, count = piece
    *outs, mark_ref, stage, sem = refs[-6:]
    mark_ref[...] = jnp.zeros_like(mark_ref)
    own = act_ref.shape[1] // slots
    base = lax.rem(scal[0] + which, n_group) * own + first
    tn = (((0,), (0,)), ((), ()))
    depth = stage.shape[0]

    def put(j, k):
        slot = lax.rem(j, depth)
        return pltpu.make_async_copy(stage.at[slot, k], outs[k].at[base + j], sem.at[slot, k])

    def step(j, carry):
        at = pl.ds(pl.multiple_of((first + j) * slots, slots), slots)
        for k, right in enumerate((xs_ref, xs_ref, gs_ref)):
            @pl.when(j >= depth)
            def _():
                put(j - depth, k).wait()

            stage[lax.rem(j, depth), k] = lax.dot_general(
                act_ref[k, at, :], right[which, at, :], tn, preferred_element_type=jnp.float32)
            put(j, k).start()
        return carry

    lax.fori_loop(0, count, step, 0)
    for j in range(max(0, count - depth), count):
        for k in range(3):
            put(j, k).wait()


def grads(scal, act, xs, gs, piece, out, after, shape, n_group, slots):
    ff, wide, count = act.shape[2], xs.shape[2], piece[2]
    depth = min(2, count)
    vmem, any_space = pl.BlockSpec(memory_space=pltpu.VMEM), pl.BlockSpec(memory_space=pl.ANY)
    return pl.pallas_call(
        functools.partial(grad_kernel, piece, slots, n_group),
        out_shape=[shape] * 3 + [jax.ShapeDtypeStruct((8, 128), jnp.float32)],
        in_specs=[pl.BlockSpec(memory_space=pltpu.SMEM)] + [vmem] * 3 + [any_space] * (4 if out else 1),
        out_specs=[any_space] * 3 + [vmem],
        scratch_shapes=[pltpu.VMEM((depth, 3, ff, wide), jnp.float32), pltpu.SemaphoreType.DMA((depth, 3))],
        input_output_aliases={5 + k: k for k in range(3)} if out else {},
        compiler_params=pltpu.CompilerParams(vmem_limit_bytes=12 << 20),
        cost_estimate=pl.CostEstimate(
            flops=count * 3 * 2 * ff * slots * wide,
            bytes_accessed=count * 3 * ff * wide * 4, transcendentals=0),
        name="weight_grads",
    )(scal, act, xs, gs, after, *(out or ()))


def swap(x, axis, bit):
    n = lax.axis_size(axis)
    return lax.ppermute(x, axis, [(k, k ^ bit) for k in range(n)])


def shards(tokens, grad_mixed, expert_ids, gate_weight, w_gate, w_up, w_down):
    tok, width = tokens.shape
    n_group, n_ingroup, n_hid = (lax.axis_size(a) for a in ("group", "ingroup", "hid"))
    exp_dev, ff = w_down.shape[0], w_down.shape[1]
    experts = exp_dev * n_hid
    cap = tok // 8
    own = exp_dev // n_group
    rows = n_group * n_hid * tok
    slots = n_group * n_hid * cap
    if not (n_group == 2 and n_ingroup == 4 and exp_dev % (2 * n_group) == 0 and n_hid & (n_hid - 1) == 0
            and rows == 128 and own * slots == 128 and 2 * experts <= 128):
        return plain(tokens, grad_mixed, expert_ids, gate_weight, w_gate, w_up, w_down)
    g, i, h = (lax.axis_index(a) for a in ("group", "ingroup", "hid"))
    scal = jnp.stack([g, i, h]).astype(jnp.int32)
    core = lax.rem(i, 2)
    half = width // 2
    table = jnp.sum(jnp.where(expert_ids[:, :, None] == jnp.arange(experts, dtype=jnp.int32)[None, None, :],
                              gate_weight[:, :, None], 0.0), axis=1)
    hi = lax.reduce_precision(table, 8, 7)
    mid = lax.reduce_precision(table - hi, 8, 7)
    low = lax.reduce_precision(table - hi - mid, 8, 7)
    zero = jnp.zeros_like(hi)
    terms = jnp.where(core == 0, jnp.concatenate([hi, mid], 1), jnp.concatenate([low, zero], 1))
    message = jnp.concatenate([
        lax.dynamic_slice_in_dim(tokens, core * half, half, 1),
        lax.dynamic_slice_in_dim(grad_mixed, core * half, half, 1),
        terms.astype(jnp.bfloat16)], axis=1)
    line = [message] + [lax.ppermute(message, "hid", [(k, (k + d) % n_hid) for k in range(n_hid)])
                        for d in range(1, n_hid)]
    messages, places = [], []
    for low in range(0, n_hid, n_hid // 2):
        group_of = range(low, low + n_hid // 2)
        mine = jnp.stack([line[d] for d in group_of])
        crossed = swap(mine, "group", 1)
        for s, block in enumerate((mine, crossed)):
            messages += [block, swap(block, "ingroup", 1)]
            places.append(tuple((s, d) for d in group_of))
    wg, wu = jnp.swapaxes(w_gate, 1, 2), jnp.swapaxes(w_up, 1, 2)
    narrow = width // n_ingroup
    any_space = pl.BlockSpec(memory_space=pl.ANY)
    vmem = pl.BlockSpec(memory_space=pltpu.VMEM)
    lanes = message.shape[1] - 2 * half
    w0 = pl.pallas_call(
        functools.partial(prefetch_kernel, own),
        out_shape=jax.ShapeDtypeStruct((4 * ff, width), jnp.bfloat16),
        in_specs=[pl.BlockSpec(memory_space=pltpu.SMEM), any_space, any_space],
        out_specs=vmem,
        scratch_shapes=[pltpu.SemaphoreType.DMA((4,))],
        compiler_params=pltpu.CompilerParams(vmem_limit_bytes=44 << 20),
        cost_estimate=pl.CostEstimate(flops=0, bytes_accessed=4 * ff * width * 2, transcendentals=0),
        name="prefetch",
    )(scal, line[-1], wg)
    keep, send, act, xs, gs = pl.pallas_call(
        functools.partial(middle_kernel, (n_group, n_ingroup, n_hid, tok, experts, half, cap), tuple(places)),
        out_shape=[
            jax.ShapeDtypeStruct((n_group * n_hid * 2, 2, tok, narrow), jnp.bfloat16),
            jax.ShapeDtypeStruct((n_group * n_hid * 2, 2, tok, narrow), jnp.bfloat16),
            jax.ShapeDtypeStruct((3, own * slots, ff), jnp.bfloat16),
            jax.ShapeDtypeStruct((n_group, own * slots, half), jnp.bfloat16),
            jax.ShapeDtypeStruct((n_group, own * slots, half), jnp.bfloat16),
        ],
        in_specs=[pl.BlockSpec(memory_space=pltpu.SMEM), vmem] + [any_space] * 3 + [vmem] * len(messages),
        out_specs=[vmem] * 5,
        scratch_shapes=[
            pltpu.VMEM((rows, width), jnp.bfloat16),
            pltpu.VMEM((rows, width), jnp.bfloat16),
            pltpu.VMEM((2, rows, lanes), jnp.float32),
            pltpu.VMEM((rows, lanes), jnp.float32),
            pltpu.VMEM((own * slots, rows), jnp.bfloat16),
            pltpu.VMEM(((3 * own - 4) * ff, width), jnp.bfloat16),
            pltpu.VMEM((3, rows, own * ff), jnp.bfloat16),
            pltpu.VMEM((rows, width), jnp.float32),
            pltpu.VMEM((rows, width), jnp.float32),
            pltpu.SemaphoreType.DMA((3, own)),
        ],
        compiler_params=pltpu.CompilerParams(vmem_limit_bytes=43 << 20),
        cost_estimate=pl.CostEstimate(flops=6 * 2 * own * ff * width * rows,
                                      bytes_accessed=3 * own * ff * width * 2, transcendentals=own * ff * rows),
        name="experts",
    )(scal, w0, wg, wu, w_down, *messages)
    grad_shape = jax.ShapeDtypeStruct((exp_dev, ff, width // n_group), jnp.float32)
    act_other = swap(act, "group", 1)
    rounds = [("ingroup", 1), ("ingroup", 2), ("group", 1)]
    bit = n_hid // 2
    while bit:
        rounds.append(("hid", bit))
        bit //= 2
    pieces = cut(own, n_group, [0] + [1] * (len(rounds) - 1))
    out, mark = None, scal
    for (axis, bit), piece in zip(rounds, pieces):
        got = swap(send, axis, bit)
        for part in piece:
            *out, mark = grads(scal, act if part[0] == 0 else act_other, xs, gs, part, out, mark, grad_shape, n_group, slots)
        keep, send = add_halves(keep, got, mark)
        mark = keep
    return (keep, send, jnp.swapaxes(out[0], 1, 2), jnp.swapaxes(out[1], 1, 2), out[2])


def cut(own, n_group, weights):
    total = own * n_group
    ends = [total * sum(weights[:k + 1]) // sum(weights) for k in range(len(weights))]
    pieces, at = [], 0
    for end in ends:
        piece = []
        while at < end:
            which, first = divmod(at, own)
            count = min(end - at, own - first)
            piece.append((which, first, count))
            at += count
        pieces.append(piece)
    return pieces


def solution(mesh):
    placed = (
        P(("group", "hid"), None),
        P(("group", "hid"), None),
        P(("group", "hid"), None),
        P(("group", "hid"), None),
        P("hid", None, "ingroup"),
        P("hid", None, "ingroup"),
        P("hid", "ingroup", None),
    )
    return jax.shard_map(
        shards,
        mesh=mesh,
        in_specs=placed,
        out_specs=(
            P(("group", "hid"), "ingroup"),
            P(("group", "hid"), "ingroup"),
            P("hid", "group", "ingroup"),
            P("hid", "group", "ingroup"),
            P("hid", "ingroup", "group"),
        ),
        check_vma=False,
    )
```
